32 devices in a mesh: seq: 8 (over y, x, core), tile: 4 (over z).
Axes of the slice: x: 2, y: 2, z: 4, core: 2. Of those that a mesh axis runs over, the one named last changes fastest.
Arguments:
- inputs: bfloat16 [8, 13, 256, 1024], P('seq', None, 'tile'), may hold values from -6 to 6
- actions: int32 [8, 13], P('seq'), may hold values from 0 to 7
- segments: int32 [8, 13], P('seq'), may hold values from 0 to 3, never falling along the last dimension, each value on 1 to 6 neighbouring positions
- cotangent: bfloat16 [8, 13, 256, 1024], P('seq', None, 'tile'), may hold values from -6 to 6
- action_table: bfloat16 [8, 1024], P(None, 'seq'), may hold values from -6 to 6
- spatial_inward: bfloat16 [1024, 3072], P('seq'), may hold values from -0.1875 to 0.1875
- spatial_outward: bfloat16 [1024, 1024], P('seq'), may hold values from -3 to 3
- temporal_inward: bfloat16 [1024, 3072], P('seq'), may hold values from -0.1875 to 0.1875
- temporal_outward: bfloat16 [1024, 1024], P('seq'), may hold values from -0.375 to 0.375
- expand_weight: bfloat16 [1024, 4096], P('seq'), may hold values from -0.1875 to 0.1875
- contract_weight: bfloat16 [4096, 1024], P('seq'), may hold values from -0.09375 to 0.09375
- expand_bias: bfloat16 [4096], P('seq'), may hold values from -3 to 3
- contract_bias: bfloat16 [1024], P('seq'), may hold values from -3 to 3
- norm_gain: bfloat16 [3, 1024], P(None, 'seq'), may hold values from 0.5 to 1.5
- norm_shift: bfloat16 [3, 1024], P(None, 'seq'), may hold values from -3 to 3
Outputs:
- outputs: bfloat16 [8, 13, 256, 1024], P('seq', None, 'tile')
- input_grad: bfloat16 [8, 13, 256, 1024], P('seq', None, 'tile')
- action_table_grad: float32 [8, 1024], P(None, 'seq')
- spatial_inward_grad: float32 [1024, 3072], P('seq')
- spatial_outward_grad: float32 [1024, 1024], P('seq')
- temporal_inward_grad: float32 [1024, 3072], P('seq')
- temporal_outward_grad: float32 [1024, 1024], P('seq')
- expand_weight_grad: float32 [1024, 4096], P('seq')
- contract_weight_grad: float32 [4096, 1024], P('seq')
- expand_bias_grad: float32 [4096], P('seq')
- contract_bias_grad: float32 [1024], P('seq')
- norm_gain_grad: float32 [3, 1024], P(None, 'seq')
- norm_shift_grad: float32 [3, 1024], P(None, 'seq')
The draws below stay inside these ranges and needn't reach their ends.
Inputs may be any that keep to these rules, and one draw needn't show every extreme that they name: Within a packed sequence the segment ids never fall from frame to frame; each sequence holds 4 segments of at most 6 frames each.
All inputs are finite; a program needn't handle non-finite values.
Results may differ from the reference program's by a relative error of at most 0.018.
Values may be sent and summed in bfloat16 or wider, within the bound.
No kernel may reach another device: no remote copies, remote signals or barrier semaphores. Data moves between devices by JAX's collectives and lax.ppermute only.
A program may use at most 320 MiB of HBM per device.

```python
import math
import jax
import jax.numpy as jnp
import numpy as np
from jax import lax

D = 1024
HEADS = 16
HEAD = 64
FF = 4096
ACTIONS = 8
FRAME = 256
FRAMES = 13
SEQS = 8


def set_ends(values, key, least, largest):
    longest = values.shape.index(max(values.shape))
    spots = []
    for shift in (0, 1):
        where = [jax.random.randint(jax.random.fold_in(key, axis), (), 0, length) for axis, length in enumerate(values.shape)]
        where[longest] = (where[longest] + shift) % values.shape[longest]
        spots.append(tuple(where))
    return values.at[spots[0]].set(least).at[spots[1]].set(largest)


def levels(own_key, dims, pieces, low, largest):
    loudness, own = 1.0, jax.random.fold_in(own_key, 6)
    for position, blocks in pieces:
        heights = jnp.exp(jax.random.uniform(jax.random.fold_in(own, position), (blocks,), jnp.float32, low / len(pieces), largest / len(pieces)))
        loudness = loudness * jnp.repeat(heights, dims[position] // blocks).reshape([-1 if axis == position else 1 for axis in range(len(dims))])
    return loudness


def split_up(count, total, most, slope):
    loads = [(1 << 20) // math.isqrt(rank ** slope) + 1 for rank in range(2, count + 1)]
    surplus, holding = total - most - (count - 1), [1] * (count - 1)
    while surplus > 0:
        free = [i for i in range(count - 1) if holding[i] < most]
        mass, budget = sum([loads[i] for i in free]), surplus
        for i in free:
            extra = min(most - holding[i], max(1, budget * loads[i] // mass), surplus)
            holding[i] = holding[i] + extra
            surplus = surplus - extra
    return np.array([most] + holding)


def uneven_parts(key, amount, total, limit, slope):
    if amount == 2:
        one = jax.random.randint(key, (), max(1, total - limit), min(limit, total - 1) + 1)
        return jnp.stack([one, total - one])
    tallies = jnp.asarray(split_up(amount, total, limit, slope), jnp.int32)
    couples = (amount - 1) // 2
    donor, sink = tallies[1:1 + 2 * couples:2], tallies[2:2 + 2 * couples:2]
    room = jnp.minimum(donor - 1, limit - sink)
    moved = jax.random.randint(jax.random.fold_in(key, 1), (couples,), 0, 1 << 20) % (room + 1)
    tallies = tallies.at[1:1 + 2 * couples:2].set(donor - moved).at[2:2 + 2 * couples:2].set(sink + moved)
    return tallies[jax.random.permutation(jax.random.fold_in(key, 2), amount)]


def gaussian(stream_key, extent, deviation, reach, cuts=(), kind=jnp.bfloat16):
    gain = levels(stream_key, extent, cuts, -0.22, 0.18) if cuts else 1.0
    values = jax.random.normal(stream_key, extent, jnp.float32) * deviation * gain
    return jnp.minimum(jnp.maximum(values, -reach), reach).astype(kind)


def setup_inputs(seed: int = 0) -> dict:
    key_list = jax.random.split(jax.random.key(seed), 16)
    return {
        "inputs": gaussian(key_list[0], (SEQS, FRAMES, FRAME, D), 1.0, 6.0, ((0, 8), (2, 4))),
        "actions": set_ends(jax.random.randint(key_list[1], (SEQS, FRAMES), 0, ACTIONS), jax.random.fold_in(key_list[1], 1), 0, ACTIONS - 1).astype(jnp.int32),
        "segments": jax.vmap(lambda own: jnp.searchsorted(jnp.cumsum(uneven_parts(own, FRAMES // 4 + 1, FRAMES, FRAMES // 2, 0)), jnp.arange(FRAMES), side="right"))(jax.random.split(key_list[2], SEQS)).reshape((SEQS, FRAMES)).astype(jnp.int32),
        "cotangent": gaussian(key_list[3], (SEQS, FRAMES, FRAME, D), 1.0, 6.0, ((0, 8), (2, 4))),
        "action_table": gaussian(key_list[4], (ACTIONS, D), 1.0, 6.0, ((1, 8),)),
        "spatial_inward": gaussian(key_list[5], (D, 3 * D), D ** -0.5, 0.1875, ((0, 8),)),
        "spatial_outward": gaussian(key_list[6], (D, D), (D // FRAME) ** -0.5, 3.0, ((0, 8),)),
        "temporal_inward": gaussian(key_list[7], (D, 3 * D), D ** -0.5, 0.1875, ((0, 8),)),
        "temporal_outward": gaussian(key_list[8], (D, D), (D // 4) ** -0.5, 0.375, ((0, 8),)),
        "expand_weight": gaussian(key_list[9], (D, FF), D ** -0.5, 0.1875, ((0, 8),)),
        "contract_weight": gaussian(key_list[10], (FF, D), FF ** -0.5, 0.09375, ((0, 8),)),
        "expand_bias": gaussian(key_list[11], (FF,), 0.5, 3.0, ((0, 8),)),
        "contract_bias": gaussian(key_list[12], (D,), 0.5, 3.0, ((0, 8),)),
        "norm_gain": jnp.clip(1.0 + 0.1 * jax.random.normal(key_list[13], (3, D), jnp.float32), 0.5, 1.5).astype(jnp.bfloat16),
        "norm_shift": gaussian(key_list[14], (3, D), 0.5, 3.0, ((1, 8),)),
    }


@jax.custom_vjp
def low(v):
    return lax.optimization_barrier(v.astype(jnp.bfloat16)).astype(jnp.float32)

@jax.custom_vjp
def low_back(v):
    return v

def low_keep(v):
    return (low(v), None)

def low_pass(kept, grad):
    return (grad,)

def back_keep(v):
    return (v, None)

def back_low(kept, grad):
    return (low(grad),)
low.defvjp(low_keep, low_pass)
low_back.defvjp(back_keep, back_low)
highest = lax.Precision.HIGHEST
epsilon = 1e-05
masked_score = -1e+30

def matmul_high(left_side, right_side):
    return jnp.matmul(left_side, right_side, precision=highest)

def layer_norm(hidden, gain_row, shift_row):
    centred = hidden - lax.optimization_barrier(jnp.mean(hidden, axis=-1, keepdims=True))
    spread = lax.optimization_barrier(jnp.mean(centred * centred, axis=-1, keepdims=True))
    return centred * lax.rsqrt(spread + epsilon) * gain_row + shift_row

def softmax_rows(scores):
    row_top = lax.optimization_barrier(jnp.max(scores, axis=-1, keepdims=True))
    powered = jnp.exp(scores - row_top)
    return powered / lax.optimization_barrier(jnp.sum(powered, axis=-1, keepdims=True))

def block_forward(sequence, params, onehot, allowed):
    table_full, space_in, space_out, time_in, time_out, expand_full, contract_full, expand_shift, contract_shift, gain_rows, shift_rows = params
    frames = sequence.shape[0]
    score_scale = HEAD ** (-0.5)
    embed_sum = sequence + matmul_high(onehot, table_full)[:, None, :]
    normed = low(layer_norm(embed_sum, gain_rows[0], shift_rows[0]))
    projected = matmul_high(normed, space_in)
    query_heads = low_back(low(projected[..., :D])).reshape(frames, FRAME, HEADS, HEAD)
    key_heads = low_back(low(projected[..., D:2 * D])).reshape(frames, FRAME, HEADS, HEAD)
    value_heads = low_back(low(projected[..., 2 * D:])).reshape(frames, FRAME, HEADS, HEAD)
    scores = low_back(jnp.einsum('fqhd,fkhd->fhqk', query_heads, key_heads, precision=highest) * score_scale)
    softmaxed = low(softmax_rows(scores))
    mixed_heads = jnp.einsum('fhqk,fkhd->fqhd', softmaxed, value_heads, precision=highest).reshape(frames, FRAME, D)
    mixed_heads = low_back(low(mixed_heads))
    space_sum = embed_sum + low_back(matmul_high(mixed_heads, space_out))
    normed = low(layer_norm(space_sum, gain_rows[1], shift_rows[1]))
    projected = matmul_high(normed, time_in)
    query_heads = low_back(low(projected[..., :D])).reshape(frames, FRAME, HEADS, HEAD)
    key_heads = low_back(low(projected[..., D:2 * D])).reshape(frames, FRAME, HEADS, HEAD)
    value_heads = low_back(low(projected[..., 2 * D:])).reshape(frames, FRAME, HEADS, HEAD)
    scores = low_back(jnp.einsum('fphd,gphd->phfg', query_heads, key_heads, precision=highest) * score_scale)
    scores = jnp.where(allowed[None, None], scores, masked_score)
    softmaxed = low(softmax_rows(scores))
    mixed_heads = jnp.einsum('phfg,gphd->fphd', softmaxed, value_heads, precision=highest).reshape(frames, FRAME, D)
    mixed_heads = low_back(low(mixed_heads))
    time_sum = space_sum + low_back(matmul_high(mixed_heads, time_out))
    normed = low(layer_norm(time_sum, gain_rows[2], shift_rows[2]))
    expanded = low_back(matmul_high(normed, expand_full) + expand_shift)
    activated = low(jax.nn.gelu(expanded, approximate=True))
    return time_sum + low_back(matmul_high(activated, contract_full)) + contract_shift

def reference(inputs, actions, segments, cotangent, action_table, spatial_inward, spatial_outward, temporal_inward, temporal_outward, expand_weight, contract_weight, expand_bias, contract_bias, norm_gain, norm_shift):
    params = tuple((weight.astype(jnp.float32) for weight in (action_table, spatial_inward, spatial_outward, temporal_inward, temporal_outward, expand_weight, contract_weight, expand_bias, contract_bias, norm_gain, norm_shift)))
    frame_index = jnp.arange(FRAMES, dtype=jnp.int32)
    action_index = jnp.arange(ACTIONS, dtype=jnp.int32)

    def one_sequence(totals, scan_items):
        sequence, action_row, segment_row, upstream = scan_items
        onehot = (action_row[:, None] == action_index[None, :]).astype(jnp.float32)
        allowed = (frame_index[None, :] <= frame_index[:, None]) & (segment_row[None, :] == segment_row[:, None])

        def forward(sequence_in, weights):
            return block_forward(sequence_in, weights, onehot, allowed)
        result, pullback = jax.vjp(forward, sequence.astype(jnp.float32), params)
        grad_input, grad_params = pullback(upstream.astype(jnp.float32))
        totals = jax.tree.map(lambda total_grad, new_grad: total_grad + new_grad, totals, grad_params)
        return (totals, (result.astype(jnp.bfloat16), grad_input.astype(jnp.bfloat16)))
    zero_grads = jax.tree.map(jnp.zeros_like, params)
    totals, stacked = lax.scan(one_sequence, zero_grads, (inputs, actions, segments, cotangent))
    return (stacked[0], stacked[1], totals[0], totals[1], totals[2], totals[3], totals[4], totals[5], totals[6], totals[7], totals[8], totals[9], totals[10])
```

```python
import functools
import math

import jax
import jax.numpy as jnp
from jax import lax
from jax.experimental import pallas as pl
from jax.experimental.pallas import tpu as pltpu
from jax.sharding import PartitionSpec as P

HEAD = 64
PAIR = 2 * HEAD
BLOCKS = 8
GROUP = 16
CHUNK = 1024
SET = 4
WIDE = 512
VMEM = 64000 * 1024

epsilon = 1e-05
masked_score = -1e30
score_scale = HEAD ** (-0.5)
f32 = jnp.float32
bf16 = jnp.bfloat16
ANY = pl.BlockSpec(memory_space=pl.ANY)


def dot_nn(left, right):
    return lax.dot_general(left, right, (((1,), (0,)), ((), ())), preferred_element_type=f32)


def dot_nt(left, right):
    return lax.dot_general(left, right, (((1,), (1,)), ((), ())), preferred_element_type=f32)


def dot_tn(left, right):
    return lax.dot_general(left, right, (((0,), (0,)), ((), ())), preferred_element_type=f32)


def flipped(block):
    return block.astype(f32).T.astype(block.dtype)


def norm_unit(hidden):
    centred = hidden - jnp.mean(hidden, axis=-1, keepdims=True)
    inverse = lax.rsqrt(jnp.mean(centred * centred, axis=-1, keepdims=True) + epsilon)
    return centred * inverse, inverse


def norm_back(upstream, unit, inverse, gain_row):
    scaled = upstream * gain_row
    mean_first = jnp.mean(scaled, axis=-1, keepdims=True)
    mean_second = jnp.mean(scaled * unit, axis=-1, keepdims=True)
    return inverse * (scaled - mean_first - unit * mean_second)


def column_sum(block):
    return jnp.sum(block, axis=0, keepdims=True)


def half_lanes(block, half):
    lanes = lax.broadcasted_iota(jnp.int32, block.shape, 1)
    return jnp.where((lanes < HEAD) == (half == 0), block, jnp.zeros_like(block))


def pair_rows(block):
    return jnp.concatenate([half_lanes(block, 0), half_lanes(block, 1)], axis=0)


def pick_lanes(stacked):
    size = stacked.shape[0] // 2
    lanes = lax.broadcasted_iota(jnp.int32, (size, stacked.shape[1]), 1)
    return jnp.where(lanes < HEAD, stacked[:size], stacked[size:])


def attend(query, key, value, mask):
    scores = dot_nt(pair_rows(query * jnp.asarray(score_scale, bf16)), key)
    if mask is not None:
        scores = jnp.where(mask, scores, masked_score)
    top = jnp.max(scores, axis=1, keepdims=True)
    powered = jnp.exp(scores - top)
    total = jnp.sum(powered, axis=1, keepdims=True)
    mixed = dot_nn(powered.astype(bf16), value) / total
    return pick_lanes(mixed).astype(bf16), top + jnp.log(total)


def attend_back(query, key, value, upstream, sums, mask):
    query = pair_rows(query * jnp.asarray(score_scale, bf16))
    upstream = pair_rows(upstream)
    scores = dot_nt(key, query)
    if mask is not None:
        scores = jnp.where(mask, scores, masked_score)
    soft = jnp.exp(scores - sums)
    grad_soft = dot_nt(value, upstream)
    inner = jnp.sum(soft * grad_soft, axis=0, keepdims=True)
    grad_scores = (soft * (grad_soft - inner)).astype(bf16)
    grad_value = dot_nn(soft.astype(bf16), upstream)
    grad_key = dot_nn(grad_scores, query)
    grad_query = pick_lanes(dot_tn(grad_scores, key)) * score_scale
    return grad_query.astype(bf16), grad_key.astype(bf16), grad_value.astype(bf16)


def lane_slices(index, width):
    base = pl.multiple_of(index * SET * PAIR, SET * PAIR)
    return [
        [pl.ds(base + (pair * PAIR + part * width), PAIR) for part in range(3)]
        for pair in range(SET)
    ]


def attend_set(index, width, load, store, mask, sums_store):
    columns = None
    for pair, lanes in enumerate(lane_slices(index, width)):
        out, sums = attend(*(load(lane) for lane in lanes), mask)
        store(lanes[0], out)
        size = out.shape[0]
        if columns is None:
            columns = jnp.zeros((size, PAIR), f32)
            spots = lax.broadcasted_iota(jnp.int32, columns.shape, 1)
        for half in (0, 1):
            part = sums[half * size : (half + 1) * size]
            columns = jnp.where(spots == 2 * pair + half, part, columns)
    sums_store(columns.T[: 2 * SET])


def attend_back_set(index, width, load, load_up, store, mask, sums):
    for pair, lanes in enumerate(lane_slices(index, width)):
        row = jnp.concatenate([sums[2 * pair : 2 * pair + 1], sums[2 * pair + 1 : 2 * pair + 2]], axis=1)
        grads = attend_back(*(load(lane) for lane in lanes), load_up(lanes[0]), row, mask)
        for lane, grad in zip(lanes, grads):
            store(lane, grad)


def piece_copies(scalars, places, refs, whole, sems, rows):
    copies = []
    for index, ((owner, offset), ref) in enumerate(zip(places, refs)):
        start = pl.multiple_of((owner ^ scalars[0]) * rows + offset, 16)
        copies.append(
            pltpu.make_async_copy(ref, whole.at[pl.ds(start, ref.shape[0])], sems.at[index])
        )
    return copies


def call(kernel, grid, in_specs, out_specs, out_shape, scratch, flops, moved, name):
    return pl.pallas_call(
        kernel,
        out_shape=out_shape,
        grid_spec=pltpu.PrefetchScalarGridSpec(
            num_scalar_prefetch=1,
            grid=grid,
            in_specs=in_specs,
            out_specs=out_specs,
            scratch_shapes=scratch,
        ),
        compiler_params=pltpu.CompilerParams(vmem_limit_bytes=VMEM),
        cost_estimate=pl.CostEstimate(flops=flops, bytes_accessed=moved, transcendentals=0),
        name=name,
    )


def shape(dims, dtype=bf16):
    return jax.ShapeDtypeStruct(tuple(dims), dtype)


def full(dims):
    return pl.BlockSpec(tuple(dims), lambda i, s: (0,) * len(dims))


def spatial_forward(scalars, tokens, embed, gain, shift, weight):
    arrays, places, rows = weight
    tiles, (frames, cells, width) = len(tokens), tokens[0].shape
    length, count = tiles * cells, len(arrays)
    heads, sets = width // HEAD, width // (PAIR * SET)

    def kernel(scalars_ref, *refs):
        token_refs, refs = refs[:tiles], refs[tiles:]
        embed_ref, gain_ref, shift_ref, *refs = refs
        pieces, refs = refs[:count], refs[count:]
        normed_ref, proj_ref, refs = refs[0], refs[1], refs[2:]
        mixed_refs, (sums_ref, whole, sems, mixed) = refs[:tiles], refs[tiles:]
        copies = piece_copies(scalars_ref, places, pieces, whole, sems, rows)
        for copy in copies:
            copy.start()
        for frame in range(frames):
            hidden = jnp.concatenate([ref[frame] for ref in token_refs], axis=0).astype(f32)
            unit, _ = norm_unit(hidden + embed_ref[frame])
            normed_ref[frame] = (unit * gain_ref[...] + shift_ref[...]).astype(bf16)
        for copy in copies:
            copy.wait()
        for start in range(0, 3 * width, CHUNK):
            part = dot_nn(rows_of(normed_ref[...]), whole[:, start : start + CHUNK])
            proj_ref[:, :, start : start + CHUNK] = part.astype(bf16).reshape(frames, length, CHUNK)

        def run(index, carry):
            frame, part = index // sets, index % sets

            def store(lane, value):
                mixed[:, lane] = value
                for tile, ref in enumerate(mixed_refs):
                    ref[frame, :, lane] = value[tile * cells : (tile + 1) * cells]

            def sums_store(value):
                spot = pl.multiple_of(part * 2 * SET, 2 * SET)
                sums_ref[frame, pl.ds(spot, 2 * SET)] = value

            attend_set(part, width, lambda lane: proj_ref[frame, :, lane], store, None, sums_store)
            return carry

        lax.fori_loop(0, frames * sets, run, 0)

    outs = call(
        kernel,
        (1,),
        [full((frames, cells, width))] * tiles
        + [full((frames, 1, width)), full((1, width)), full((1, width))]
        + [ANY] * count,
        [full((frames, length, width)), full((frames, length, 3 * width))]
        + [full((frames, cells, width))] * tiles
        + [full((frames, heads, length))],
        [shape((frames, length, width)), shape((frames, length, 3 * width))]
        + [shape((frames, cells, width))] * tiles
        + [shape((frames, heads, length), f32)],
        [
            pltpu.VMEM((width, 3 * width), bf16),
            pltpu.SemaphoreType.DMA((count,)),
            pltpu.VMEM((length, width), bf16),
        ],
        2 * frames * length * width * (3 * width + 2 * length) * 2,
        20 << 20,
        "spatial_forward",
    )(scalars, *tokens, embed, gain, shift, *arrays)
    return outs[0], outs[1], outs[2 : 2 + tiles], outs[2 + tiles]


def spatial_backward(scalars, upstreams, tokens, embed, gain, proj, sums, weight):
    arrays, places, rows = weight
    tiles, (frames, cells, width) = len(tokens), tokens[0].shape
    length, count = tiles * cells, len(arrays)
    heads, sets = width // HEAD, width // (PAIR * SET)

    def kernel(scalars_ref, *refs):
        up_refs, refs = refs[:tiles], refs[tiles:]
        token_refs, refs = refs[:tiles], refs[tiles:]
        embed_ref, gain_ref, proj_ref, sums_ref, *refs = refs
        pieces, refs = refs[:count], refs[count:]
        grad_ref, refs = refs[0], refs[1:]
        back_refs, refs = refs[:tiles], refs[tiles:]
        gain_grad, shift_grad, frame_sum, whole, sems, upstream = refs
        copies = piece_copies(scalars_ref, places, pieces, whole, sems, rows)
        for copy in copies:
            copy.start()
        for tile, ref in enumerate(up_refs):
            upstream[:, tile * cells : (tile + 1) * cells] = ref[...]

        def run(index, carry):
            frame, part = index // sets, index % sets

            def store(lane, value):
                grad_ref[frame, :, lane] = value

            spot = pl.multiple_of(part * 2 * SET, 2 * SET)
            attend_back_set(
                part,
                width,
                lambda lane: proj_ref[frame, :, lane],
                lambda lane: upstream[frame, :, lane],
                store,
                None,
                sums_ref[frame, pl.ds(spot, 2 * SET)],
            )
            return carry

        lax.fori_loop(0, frames * sets, run, 0)
        for copy in copies:
            copy.wait()
        grad_normed = dot_nt(rows_of(grad_ref[...]), whole[...])
        gains, shifts = 0, 0
        for frame in range(frames):
            hidden = jnp.concatenate([ref[frame] for ref in token_refs], axis=0).astype(f32)
            unit, inverse = norm_unit(hidden + embed_ref[frame])
            grad = grad_normed[frame * length : (frame + 1) * length]
            back = norm_back(grad, unit, inverse, gain_ref[...])
            gains, shifts = gains + column_sum(grad * unit), shifts + column_sum(grad)
            frame_sum[frame] = column_sum(back)
            for tile, ref in enumerate(back_refs):
                ref[frame] = back[tile * cells : (tile + 1) * cells].astype(bf16)
        gain_grad[...], shift_grad[...] = gains, shifts

    tile_spec = full((frames, cells, width))
    outs = call(
        kernel,
        (1,),
        [tile_spec] * (2 * tiles)
        + [full((frames, 1, width)), full((1, width)), full((frames, length, 3 * width))]
        + [full((frames, heads, length))]
        + [ANY] * count,
        [full((frames, length, 3 * width))]
        + [tile_spec] * tiles
        + [full((1, width)), full((1, width)), full((frames, 1, width))],
        [shape((frames, length, 3 * width))]
        + [shape((frames, cells, width))] * tiles
        + [shape((1, width), f32)] * 2
        + [shape((frames, 1, width), f32)],
        [
            pltpu.VMEM((width, 3 * width), bf16),
            pltpu.SemaphoreType.DMA((count,)),
            pltpu.VMEM((frames, length, width), bf16),
        ],
        2 * frames * length * width * (3 * width + 5 * length) * 2,
        24 << 20,
        "spatial_backward",
    )(scalars, *upstreams, *tokens, embed, gain, proj, sums, *arrays)
    return outs[0], outs[1 : 1 + tiles], outs[1 + tiles], outs[2 + tiles], outs[3 + tiles]


def rows_of(block):
    return block.reshape(block.shape[0] * block.shape[1], block.shape[2])


def temporal_forward(scalars, tokens, embed, mixed_parts, share, gains, shifts, mask, weight):
    arrays, places, rows = weight
    frames, cells, width = tokens.shape
    tiles, count = len(mixed_parts[0][0]), len(arrays)
    parts = [(array, tile, first) for part, first in mixed_parts for tile, array in enumerate(part)]
    heads, sets, size = width // HEAD, width // (PAIR * SET), frames * GROUP
    groups = cells // GROUP

    def kernel(scalars_ref, *refs):
        token_ref, embed_ref, *refs = refs
        part_refs, refs = refs[: len(parts)], refs[len(parts) :]
        gain_ref, shift_ref, mask_ref, *refs = refs
        pieces, refs = refs[:count], refs[count:]
        outs, kept, (sums_ref,), refs = refs[:7], refs[8:15], refs[7:8], refs[15:]
        whole, sems, gathered, out_sems = refs
        space, first, normed, proj, mixed, second, last = kept
        copies = piece_copies(scalars_ref, places, pieces, whole, sems, rows)
        flushes = [
            pltpu.make_async_copy(ref, out, out_sems.at[index])
            for index, (ref, out) in enumerate(zip(kept, outs))
        ]
        for copy in copies:
            copy.start()
        for ref, (_, tile, start) in zip(part_refs, parts):
            spot = (tile ^ scalars_ref[1]) * share + start
            gathered[pl.ds(spot, ref.shape[0])] = ref[...]
        space[...] = gathered[:frames]
        flushes[0].start()
        for copy in copies:
            copy.wait()
        hidden = rows_of(token_ref[...].astype(f32) + embed_ref[...])
        hidden = hidden + dot_nn(rows_of(space[...]), whole[:, :width])
        first[...] = hidden.reshape(first.shape)
        flushes[1].start()
        unit, _ = norm_unit(hidden)
        normed[...] = (unit * gain_ref[1:2] + shift_ref[1:2]).astype(bf16).reshape(normed.shape)
        flushes[2].start()
        for start in range(0, 3 * width, CHUNK):
            part = dot_nn(rows_of(normed[...]), whole[:, width + start : width + start + CHUNK])
            proj[:, :, start : start + CHUNK] = part.astype(bf16).reshape(frames, cells, CHUNK)
        flushes[3].start()
        allowed = mask_ref[...] > 0

        def run(index, carry):
            group, part = index // sets, index % sets
            places_here = pl.ds(pl.multiple_of(group * GROUP, GROUP), GROUP)

            def store(lane, value):
                mixed[:, places_here, lane] = value.reshape(frames, GROUP, PAIR)

            def sums_store(value):
                spot = pl.multiple_of(part * 2 * SET, 2 * SET)
                sums_ref[group, pl.ds(spot, 2 * SET)] = value

            attend_set(
                part,
                width,
                lambda lane: rows_of(proj[:, places_here, lane]),
                store,
                allowed,
                sums_store,
            )
            return carry

        lax.fori_loop(0, groups * sets, run, 0)
        flushes[4].start()
        hidden = rows_of(first[...]) + dot_nn(rows_of(mixed[...]), whole[:, 4 * width :])
        second[...] = hidden.reshape(second.shape)
        flushes[5].start()
        unit, _ = norm_unit(hidden)
        last[...] = (unit * gain_ref[2:3] + shift_ref[2:3]).astype(bf16).reshape(last.shape)
        flushes[6].start()
        for flush in flushes:
            flush.wait()

    wide = (frames, cells, width)
    kept = [
        (wide, bf16),
        (wide, f32),
        (wide, bf16),
        ((frames, cells, 3 * width), bf16),
        (wide, bf16),
        (wide, f32),
        (wide, bf16),
    ]
    return call(
        kernel,
        (1,),
        [full(wide), full((frames, 1, width))]
        + [full(array.shape) for array, _, _ in parts]
        + [full((3, width)), full((3, width)), full((2 * size, size))]
        + [ANY] * count,
        [ANY] * 7 + [full((groups, heads, size))],
        [shape(*k) for k in kept] + [shape((groups, heads, size), f32)],
        [pltpu.VMEM(*k) for k in kept]
        + [
            pltpu.VMEM((width, 5 * width), bf16),
            pltpu.SemaphoreType.DMA((count,)),
            pltpu.VMEM((share * tiles, cells, width), bf16),
            pltpu.SemaphoreType.DMA((7,)),
        ],
        2 * frames * cells * width * (5 * width + 2 * size) * 2,
        40 << 20,
        "temporal_forward",
    )(scalars, tokens, embed, *[p[0] for p in parts], gains, shifts, mask, *arrays)


def temporal_backward(
    scalars, upstream, upstream_low, hidden, proj, sums, gains, mask, weight, tiles, share, splits
):
    arrays, places, rows = weight
    frames, cells, width = upstream.shape
    count = len(arrays)
    heads, sets, size = width // HEAD, width // (PAIR * SET), frames * GROUP
    groups = cells // GROUP
    parts = [(tile, start, many) for start, many in splits for tile in range(tiles)]

    def kernel(scalars_ref, *refs):
        up_ref, low_ref, hidden_ref, proj_ref, sums_ref, gain_ref, mask_ref, *refs = refs
        pieces, refs = refs[:count], refs[count:]
        grad_out, first_out, low_out, *refs = refs
        space_refs, refs = refs[: len(parts)], refs[len(parts) :]
        gain_grad, shift_grad, frame_sum, grads, first, first_low, *refs = refs
        whole, sems, mixed, spread, out_sems = refs
        copies = piece_copies(scalars_ref, places, pieces, whole, sems, rows)
        flushes = [
            pltpu.make_async_copy(ref, out, out_sems.at[index])
            for index, (ref, out) in enumerate(
                ((grads, grad_out), (first, first_out), (first_low, low_out))
            )
        ]
        for copy in copies:
            copy.start()
        spread[frames:] = jnp.zeros((spread.shape[0] - frames, cells, width), bf16)
        for copy in copies:
            copy.wait()
        part = dot_nt(rows_of(low_ref[...]), whole[:, 4 * width :])
        mixed[...] = part.astype(bf16).reshape(mixed.shape)
        allowed = mask_ref[...] > 0

        def run(index, carry):
            group, part = index // sets, index % sets
            places_here = pl.ds(pl.multiple_of(group * GROUP, GROUP), GROUP)

            def store(lane, value):
                grads[:, places_here, lane] = value.reshape(frames, GROUP, PAIR)

            spot = pl.multiple_of(part * 2 * SET, 2 * SET)
            attend_back_set(
                part,
                width,
                lambda lane: rows_of(proj_ref[:, places_here, lane]),
                lambda lane: rows_of(mixed[:, places_here, lane]),
                store,
                allowed,
                sums_ref[group, pl.ds(spot, 2 * SET)],
            )
            return carry

        lax.fori_loop(0, groups * sets, run, 0)
        flushes[0].start()
        grad_normed = dot_nt(rows_of(grads[...]), whole[:, width : 4 * width])
        unit, inverse = norm_unit(rows_of(hidden_ref[...]))
        gain_grad[...] = column_sum(grad_normed * unit)
        shift_grad[...] = column_sum(grad_normed)
        out = rows_of(up_ref[...]) + norm_back(grad_normed, unit, inverse, gain_ref[1:2])
        out = out.reshape(first.shape)
        first[...] = out
        first_low[...] = out.astype(bf16)
        flushes[1].start()
        flushes[2].start()
        frame_sum[...] = jnp.sum(out, axis=1, keepdims=True)
        space = dot_nt(rows_of(first_low[...]), whole[:, :width]).astype(bf16)
        spread[:frames] = space.reshape(frames, cells, width)
        for ref, (tile, start, many) in zip(space_refs, parts):
            spot = (tile ^ scalars_ref[1]) * share + start
            ref[...] = spread[pl.ds(spot, many)]
        for flush in flushes:
            flush.wait()

    wide = (frames, cells, width)
    kept = [((frames, cells, 3 * width), bf16), (wide, f32), (wide, bf16)]
    outs = call(
        kernel,
        (1,),
        [full(wide)] * 3
        + [full((frames, cells, 3 * width)), full((groups, heads, size))]
        + [full((3, width)), full((size, 2 * size))]
        + [ANY] * count,
        [ANY] * 3
        + [full((many, cells, width)) for _, _, many in parts]
        + [full((1, width)), full((1, width)), full((frames, 1, width))],
        [shape(*k) for k in kept]
        + [shape((many, cells, width)) for _, _, many in parts]
        + [shape((1, width), f32)] * 2
        + [shape((frames, 1, width), f32)],
        [pltpu.VMEM(*k) for k in kept]
        + [
            pltpu.VMEM((width, 5 * width), bf16),
            pltpu.SemaphoreType.DMA((count,)),
            pltpu.VMEM(wide, bf16),
            pltpu.VMEM((max(share * tiles, frames + 1), cells, width), bf16),
            pltpu.SemaphoreType.DMA((3,)),
        ],
        2 * frames * cells * width * (5 * width + 5 * size) * 2,
        40 << 20,
        "temporal_backward",
    )(scalars, upstream, upstream_low, hidden, proj, sums, gains, mask, *arrays)
    ups = outs[3 : 3 + len(parts)]
    ups = [ups[i : i + tiles] for i in range(0, len(parts), tiles)]
    return outs[0], outs[1], outs[2], ups, *outs[3 + len(parts) :]


def expand_forward(scalars, normed, bias, weight):
    arrays, places, rows = weight
    size, width = normed.shape
    hidden, count = arrays[0].shape[1], len(arrays)
    root = math.sqrt(2 / math.pi)

    def kernel(scalars_ref, normed_ref, bias_ref, *refs):
        pieces, (act_ref, slope_ref, whole) = refs[:count], refs[count:]
        for (owner, offset), ref in zip(places, pieces):
            start = pl.multiple_of((owner ^ scalars_ref[0]) * rows + offset, 16)
            whole[pl.ds(start, ref.shape[0])] = ref[...]
        value = dot_nn(normed_ref[...], whole[...]) + bias_ref[...]
        square = value * value
        gate = 0.5 + 0.5 * jnp.tanh(value * (root + (root * 0.044715) * square))
        act = value * gate
        act_ref[...] = act.astype(bf16)
        slope = gate + act * (1.0 - gate) * (2 * root + (6 * root * 0.044715) * square)
        slope_ref[...] = slope.astype(bf16)

    out_spec = pl.BlockSpec((size, WIDE), lambda n, s: (0, n))
    return call(
        kernel,
        (hidden // WIDE,),
        [
            pl.BlockSpec((size, width), lambda n, s: (0, 0)),
            pl.BlockSpec((1, WIDE), lambda n, s: (0, n)),
        ]
        + [pl.BlockSpec((array.shape[0], WIDE), lambda n, s: (0, n)) for array in arrays],
        [out_spec, out_spec],
        [shape((size, hidden)), shape((size, hidden))],
        [pltpu.VMEM((width, WIDE), bf16)],
        2 * size * width * hidden,
        25 << 20,
        "expand_forward",
    )(scalars, normed, bias, *arrays)


def half_pieces(places, step, count):
    if count == 1:
        return [0] if step == 0 else []
    return [i for i, (owner, _) in enumerate(places) if owner // 2 == step]


def expand_backward(scalars, upstream, slope, hidden, gain, expand, contract):
    arrays, places, rows = expand
    arrays_c, places_c, rows_c = contract
    size, width = upstream.shape
    inner, count, count_c = slope.shape[1], len(arrays), len(arrays_c)
    steps = BLOCKS // 2
    chunk = inner // steps

    def kernel(scalars_ref, up_ref, slope_ref, hidden_ref, gain_ref, *refs):
        pieces, refs = refs[:count], refs[count:]
        pieces_c, refs = refs[:count_c], refs[count_c:]
        grad_ref, out_ref, low_ref, gain_grad, shift_grad, bias_grad, out_bias, *refs = refs
        whole, sems, whole_c, sems_c, total = refs
        step = pl.program_id(0)

        def columns(spot):
            start = pl.multiple_of((spot ^ (scalars_ref[0] // 2)) * chunk, chunk)
            return pl.ds(start, chunk)

        copies_c = piece_copies(scalars_ref, places_c, pieces_c, whole_c, sems_c, rows_c)
        copies = []
        for spot in range(steps):
            lanes = columns(spot)
            copies.append(
                piece_copies(
                    scalars_ref,
                    places,
                    [ref.at[:, lanes] for ref in pieces],
                    whole.at[:, lanes],
                    sems.at[spot],
                    rows,
                )
            )

        @pl.when(step == 0)
        def _():
            for spot in range(steps):
                for index in half_pieces(places_c, spot, count_c):
                    copies_c[index].start()
                for copy in copies[spot]:
                    copy.start()
            total[...] = jnp.zeros_like(total)

        for spot in range(steps):

            @pl.when(step == spot)
            def _(spot=spot):
                for index in half_pieces(places_c, spot, count_c):
                    copies_c[index].wait()
                for copy in copies[spot]:
                    copy.wait()

        lanes = columns(step)
        grad = dot_nt(up_ref[...], whole_c[lanes]) * slope_ref[...].astype(f32)
        grad_ref[...] = grad.astype(bf16)
        bias_grad[...] = column_sum(grad)
        total[...] += dot_nt(grad_ref[...], whole[:, lanes])

        @pl.when(step == steps - 1)
        def _():
            unit, inverse = norm_unit(hidden_ref[...])
            gain_grad[...] = column_sum(total[...] * unit)
            shift_grad[...] = column_sum(total[...])
            up = up_ref[...].astype(f32)
            out_bias[...] = column_sum(up)
            out = up + norm_back(total[...], unit, inverse, gain_ref[2:3])
            out_ref[...] = out
            low_ref[...] = out.astype(bf16)

    def part_spec(lines):
        return pl.BlockSpec((lines, chunk), lambda n, s: (0, n ^ (s[0] // 2)))

    once = pl.Buffered(1)
    return call(
        kernel,
        (steps,),
        [
            pl.BlockSpec((size, width), lambda n, s: (0, 0), pipeline_mode=once),
            part_spec(size),
            pl.BlockSpec((size, width), lambda n, s: (0, 0), pipeline_mode=once),
            full((3, width)),
        ]
        + [ANY] * (count + count_c),
        [part_spec(size), full((size, width)), full((size, width))]
        + [full((1, width)), full((1, width)), part_spec(1), full((1, width))],
        [
            shape((size, inner)),
            shape((size, width), f32),
            shape((size, width)),
            shape((1, width), f32),
            shape((1, width), f32),
            shape((1, inner), f32),
            shape((1, width), f32),
        ],
        [
            pltpu.VMEM((width, inner), bf16),
            pltpu.SemaphoreType.DMA((steps, count)),
            pltpu.VMEM((inner, width), bf16),
            pltpu.SemaphoreType.DMA((count_c,)),
            pltpu.VMEM((size, width), f32),
        ],
        4 * size * width * inner,
        40 << 20,
        "expand_backward",
    )(scalars, upstream, slope, hidden, gain, *arrays, *arrays_c)


def contract_forward(scalars, act, hidden, bias, contract):
    arrays, places, rows = contract
    size, inner = act.shape
    width, count = hidden.shape[1], len(arrays)
    steps = BLOCKS // 2
    chunk = inner // steps

    def kernel(scalars_ref, act_ref, hidden_ref, bias_ref, *refs):
        pieces, (out_ref, whole, sems, total) = refs[:count], refs[count:]
        step = pl.program_id(0)
        copies = piece_copies(scalars_ref, places, pieces, whole, sems, rows)

        @pl.when(step == 0)
        def _():
            for spot in range(steps):
                for index in half_pieces(places, spot, count):
                    copies[index].start()
            total[...] = hidden_ref[...] + bias_ref[...]

        for spot in range(steps):

            @pl.when(step == spot)
            def _(spot=spot):
                for index in half_pieces(places, spot, count):
                    copies[index].wait()

        lines = pl.ds(pl.multiple_of((step ^ (scalars_ref[0] // 2)) * chunk, chunk), chunk)
        total[...] += dot_nn(act_ref[...], whole[lines])

        @pl.when(step == steps - 1)
        def _():
            out_ref[...] = total[...].astype(bf16)

    return call(
        kernel,
        (steps,),
        [
            pl.BlockSpec((size, chunk), lambda n, s: (0, n ^ (s[0] // 2))),
            full((size, width)),
            full((1, width)),
        ]
        + [ANY] * count,
        [full((size, width))],
        [shape((size, width))],
        [
            pltpu.VMEM((inner, width), bf16),
            pltpu.SemaphoreType.DMA((count,)),
            pltpu.VMEM((size, width), f32),
        ],
        2 * size * width * inner,
        20 << 20,
        "contract_forward",
    )(scalars, act, hidden, bias, *arrays)[0]


def weight_grad(scalars, left, right, name):
    size, height = left.shape
    width = right.shape[1]
    rows, half = height // BLOCKS, BLOCKS // 2
    outs = [shape((half * rows, width))] * 2
    cost = (2 * size * height * width, (size * (height + width) + height * width) * 2, name)
    if rows >= 512:

        def kernel(scalars_ref, keep_left, send_left, right_ref, keep_ref, send_ref):
            keep_ref[...] = dot_tn(keep_left[...], right_ref[...]).astype(bf16)
            send_ref[...] = dot_tn(send_left[...], right_ref[...]).astype(bf16)

        def left_spec(flip):
            return pl.BlockSpec((size, rows), lambda j, s: (0, (2 * j + flip) ^ s[0]))

        out_spec = pl.BlockSpec((rows, width), lambda j, s: (j, 0))
        right_spec = pl.BlockSpec((size, width), lambda j, s: (0, 0))
        specs = [left_spec(0), left_spec(1), right_spec]
        return call(kernel, (half,), specs, [out_spec] * 2, outs, [], *cost)(
            scalars, left, left, right
        )

    chunk = min(CHUNK, width)

    def kernel(scalars_ref, left_ref, right_ref, keep_ref, send_ref, turned):
        @pl.when(pl.program_id(0) == 0)
        def _():
            for spot in range(BLOCKS):
                owner = 2 * (spot % half) + spot // half
                lanes = pl.ds(pl.multiple_of((owner ^ scalars_ref[0]) * rows, rows), rows)
                turned[spot * rows : (spot + 1) * rows] = flipped(left_ref[:, lanes])

        out = dot_nn(turned[...], right_ref[...]).astype(bf16)
        keep_ref[...] = out[: half * rows]
        send_ref[...] = out[half * rows :]

    out_spec = pl.BlockSpec((half * rows, chunk), lambda n, s: (0, n))
    return call(
        kernel,
        (width // chunk,),
        [
            pl.BlockSpec((size, height), lambda n, s: (0, 0)),
            pl.BlockSpec((size, chunk), lambda n, s: (0, n)),
        ],
        [out_spec, out_spec],
        outs,
        [pltpu.VMEM((height, size), bf16)],
        *cost,
    )(scalars, left, right)


def input_back(scalars, upstream, back_parts, share):
    frames, cells, width = upstream.shape
    tiles = len(back_parts[0][0])
    parts = [(array, tile, first) for part, first in back_parts for tile, array in enumerate(part)]

    def kernel(scalars_ref, up_ref, *refs):
        part_refs, (out_ref, gathered) = refs[: len(parts)], refs[len(parts) :]
        for ref, (_, tile, start) in zip(part_refs, parts):
            spot = (tile ^ scalars_ref[1]) * share + start
            gathered[pl.ds(spot, ref.shape[0])] = ref[...]
        out_ref[...] = (up_ref[...] + gathered[:frames].astype(f32)).astype(bf16)

    def spec(lines):
        return pl.BlockSpec((lines, GROUP, width), lambda g, s: (0, g, 0))

    return call(
        kernel,
        (cells // GROUP,),
        [spec(frames)] + [spec(array.shape[0]) for array, _, _ in parts],
        [spec(frames)],
        [shape(upstream.shape)],
        [pltpu.VMEM((share * tiles, GROUP, width), bf16)],
        0,
        8 * frames * cells * width,
        "input_back",
    )(scalars, upstream, *[p[0] for p in parts])[0]


CORE, XCHIP, YCHIP = 1, 2, 4


def gate(value, *after):
    return lax.optimization_barrier((value, after))[0]


def across(array, flip):
    return lax.ppermute(array, "seq", [(i, i ^ flip) for i in range(BLOCKS)])


def gather_pieces(shard, after=()):
    half = shard.shape[0] // 2
    shard = gate(shard, *after)
    from_x, from_y = across(shard, XCHIP), across(shard, YCHIP)
    far_low = across(from_y[:half], XCHIP)
    far_high = across(from_x[half:], YCHIP)
    mine = [
        (shard, 0, 0),
        (from_x, XCHIP, 0),
        (from_y, YCHIP, 0),
        (far_low, XCHIP | YCHIP, 0),
        (far_high, XCHIP | YCHIP, half),
    ]
    theirs = [(across(array, CORE), owner | CORE, offset) for array, owner, offset in mine]
    pieces = mine + theirs
    weight = ([p[0] for p in pieces], [p[1:] for p in pieces], shard.shape[0])
    return weight, (from_x, from_y), (far_low, far_high)


class SeqSum:
    def __init__(self, keep, send):
        self.cut = (2, 2, 2, keep.shape[0] // 8, keep.shape[1])
        self.keep, self.received = keep.reshape(self.cut), across(send, CORE).reshape(self.cut)

    def both(self, index):
        return self.keep[index].astype(f32) + self.received[index].astype(f32)

    def first(self):
        send_x = self.both((slice(None), 1, 0)).astype(bf16)
        send_y = self.both((1, slice(None), 1)).astype(bf16)
        self.from_x, self.from_y = across(send_x, XCHIP), across(send_y, YCHIP)
        return send_x, send_y

    def second(self):
        send_y = (self.both((1, 0, 0)) + self.from_x[1].astype(f32)).astype(bf16)
        send_x = (self.both((0, 1, 1)) + self.from_y[1].astype(f32)).astype(bf16)
        self.low, self.high = across(send_y, YCHIP), across(send_x, XCHIP)
        return send_x, send_y

    def total(self):
        low = self.both((0, 0, 0)) + self.from_x[0].astype(f32) + self.low.astype(f32)
        high = self.both((0, 0, 1)) + self.from_y[0].astype(f32) + self.high.astype(f32)
        return jnp.concatenate([low, high], axis=0).astype(bf16)


class LineSum:
    def __init__(self, block):
        self.block, self.sum, self.hop = block, block.astype(f32), 0
        self.up = self.down = block

    def step(self):
        last = lax.axis_size("tile") - 1
        up = lax.ppermute(self.up, "tile", [(self.hop, self.hop + 1)])
        down = lax.ppermute(self.down, "tile", [(last - self.hop, last - self.hop - 1)])
        self.hop += 1
        self.sum = self.sum + up.astype(f32) + down.astype(f32)
        self.up = (self.block.astype(f32) + up.astype(f32)).astype(bf16)
        self.down = (self.block.astype(f32) + down.astype(f32)).astype(bf16)
        return up, down


def plain_total(keep, send):
    width, rows = keep.shape[1], keep.shape[0] // (BLOCKS // 2)
    cut = (BLOCKS // 2, rows, width)
    whole = jnp.stack([keep.reshape(cut), send.reshape(cut)], axis=1).reshape(-1, width)
    shard = lax.psum_scatter(whole, "seq", scatter_dimension=0, tiled=True)
    return lax.psum(shard, "tile").astype(f32)


def exchange(chunks, direct):
    if direct:
        count = len(chunks)
        return [chunks[0]] + [
            lax.ppermute(chunks[k], "tile", [(i, i ^ k) for i in range(count)])
            for k in range(1, count)
        ]
    mixed = lax.all_to_all(jnp.stack(chunks), "tile", 0, 0)
    return [mixed[k] for k in range(len(chunks))]


def sum_everywhere(array):
    for flip in (CORE, XCHIP, YCHIP):
        array = array + across(array, flip)
    for flip in (1, 2):
        array = array + lax.ppermute(array, "tile", [(i, i ^ flip) for i in range(4)])
    return array


def body(
    inputs,
    actions,
    segments,
    cotangent,
    action_table,
    spatial_inward,
    spatial_outward,
    temporal_inward,
    temporal_outward,
    expand_weight,
    contract_weight,
    expand_bias,
    contract_bias,
    norm_gain,
    norm_shift,
):
    seqs, tiles = lax.axis_size("seq"), lax.axis_size("tile")
    direct = seqs == BLOCKS and tiles == 4
    _, frames, cells, width = inputs.shape
    share = -(-frames // tiles)
    splits = [(0, share // 2), (share // 2, share // 2)] if share % 2 == 0 else [(0, share)]
    kinds = action_table.shape[0]
    lanes = action_table.shape[1]
    me = lax.axis_index("seq").astype(jnp.int32) if direct else jnp.int32(0)
    spot = lax.axis_index("tile").astype(jnp.int32)
    scalars = jnp.stack([me, spot if direct else jnp.int32(0)])

    tokens = inputs[0]
    padded = jnp.pad(tokens, ((0, share * tiles - frames), (0, 0), (0, 0)))
    frame_tokens = []
    for first, many in splits:
        chunks = [
            lax.dynamic_slice_in_dim(padded, (spot ^ k if direct else k) * share + first, many, 0)
            for k in range(tiles)
        ]
        frame_tokens.append(exchange(chunks, direct))

    small = jnp.concatenate(
        [
            action_table,
            norm_gain,
            norm_shift,
            expand_bias.reshape(-1, lanes),
            contract_bias.reshape(1, lanes),
        ],
        axis=0,
    )
    small = lax.all_gather(small, "seq", axis=0)
    small = small.astype(f32)

    def joined(start, stop):
        return small[:, start:stop].transpose(1, 0, 2).reshape(stop - start, -1)

    table = joined(0, kinds)
    gains = joined(kinds, kinds + 3)
    shifts = joined(kinds + 3, kinds + 6)
    wide_bias = small[:, kinds + 6 : -1].reshape(1, -1)
    out_bias = small[:, -1].reshape(1, -1)

    middle = jnp.concatenate([spatial_outward, temporal_inward, temporal_outward], axis=1)
    if direct:
        space_in, near_one, far_one = gather_pieces(spatial_inward)
        middle, near_two, far_two = gather_pieces(middle, near_one)
        expand, near_three, far_three = gather_pieces(expand_weight, near_two)
        contract, near_four, far_four = gather_pieces(contract_weight, near_three)
    else:
        near_one = near_two = near_three = near_four = ()
        far_one = far_two = far_three = far_four = ()
        space_in, middle, expand, contract = (
            ([whole], [(0, 0)], whole.shape[0] // BLOCKS)
            for whole in (
                lax.all_gather(shard, "seq", axis=0, tiled=True)
                for shard in (spatial_inward, middle, expand_weight, contract_weight)
            )
        )

    onehot = (actions[0][:, None] == jnp.arange(kinds, dtype=jnp.int32)[None, :]).astype(f32)
    embed = jnp.dot(onehot, table, precision=lax.Precision.HIGHEST)
    onehot_own = lax.dynamic_slice_in_dim(
        jnp.pad(onehot, ((0, share * tiles - frames), (0, 0))), spot * share, share, 0
    )
    embed_own = jnp.dot(onehot_own, table, precision=lax.Precision.HIGHEST)
    embed, embed_own = embed[:, None, :], embed_own[:, None, :]

    index = jnp.arange(frames * GROUP, dtype=jnp.int32)
    frame_of, place_of = index // GROUP, index % GROUP
    ids = jnp.repeat(segments[0], GROUP)
    mask = (
        (place_of[:, None] == place_of[None, :])
        & (frame_of[:, None] >= frame_of[None, :])
        & (ids[:, None] == ids[None, :])
    ).astype(f32)
    mask_rows = jnp.concatenate([mask, mask], axis=0)
    mask_lanes = jnp.concatenate([mask.T, mask.T], axis=1)

    saved, mixed_parts = [], []
    waits = [near_one, near_two]
    for part, (first, many) in enumerate(splits):
        normed, proj, mixed, sums = spatial_forward(
            gate(scalars, *waits[part]),
            frame_tokens[part],
            embed_own[first : first + many],
            gains[0:1],
            shifts[0:1],
            space_in,
        )
        saved.append((normed, proj, sums))
        mixed_parts.append((exchange(list(mixed), direct), first))
    (
        space_rows,
        space_sum,
        normed_two,
        time_proj,
        time_mixed,
        time_sum,
        normed_three,
        time_sums,
    ) = temporal_forward(
        gate(scalars, *near_three),
        tokens,
        embed,
        mixed_parts,
        share,
        gains,
        shifts,
        mask_rows,
        middle,
    )

    def flat(array):
        return array.reshape(-1, array.shape[-1])

    upstream = flat(cotangent[0])
    act, slope = expand_forward(
        gate(scalars, *near_four), flat(normed_three), wide_bias, expand
    )
    contract_parts = weight_grad(gate(scalars, *far_four), act, upstream, "contract_grad")
    if direct:
        contract_sum = SeqSum(*contract_parts)
    (
        grad_hidden,
        grad_time_sum,
        time_low,
        gain_three,
        shift_three,
        grad_wide_bias,
        grad_out_bias,
    ) = expand_backward(scalars, upstream, slope, flat(time_sum), gains, expand, contract)

    after = contract_sum.first() if direct else ()
    expand_parts = weight_grad(
        gate(scalars, *after), flat(normed_three), grad_hidden, "expand_grad"
    )
    if direct:
        expand_sum = SeqSum(*expand_parts)
    outputs = contract_forward(
        gate(scalars, *expand_parts), act, flat(time_sum), out_bias, contract
    )

    after = (outputs,)
    if direct:
        after = (outputs, *contract_sum.second(), *expand_sum.first())
    (
        grad_time_proj,
        grad_space_sum,
        space_low,
        space_ups,
        gain_two,
        shift_two,
        frame_sum,
    ) = temporal_backward(
        gate(scalars, *after),
        grad_time_sum.reshape(frames, cells, width),
        time_low.reshape(frames, cells, width),
        space_sum,
        time_proj,
        time_sums,
        gains,
        mask_lanes,
        middle,
        tiles,
        share,
        splits,
    )
    frame_ups = [exchange(list(ups), direct) for ups in space_ups]
    after = (grad_time_proj,)
    if direct:
        contract_line = LineSum(contract_sum.total())
        after = (grad_time_proj, *expand_sum.second(), contract_line.block)
    time_in_parts = weight_grad(
        gate(scalars, *after), flat(normed_two), flat(grad_time_proj), "time_in_grad"
    )
    after = time_in_parts
    if direct:
        time_in_sum = SeqSum(*time_in_parts)
        expand_line = LineSum(expand_sum.total())
        after = (*time_in_parts, *contract_line.step(), expand_line.block)
    time_out_parts = weight_grad(gate(scalars, *after), flat(time_mixed), time_low, "time_out_grad")
    space_out_parts = weight_grad(
        gate(scalars, *time_out_parts), flat(space_rows), flat(space_low), "space_out_grad"
    )
    out_parts = [
        jnp.concatenate(pair, axis=1) for pair in zip(time_out_parts, space_out_parts)
    ]
    after = (*space_out_parts,)
    if direct:
        out_sum = SeqSum(*out_parts)
        after = (*space_out_parts, *time_in_sum.first())

    back_parts, grad_space_parts = [], []
    gain_one = shift_one = 0
    own_sums = []
    for part, (first, many) in enumerate(splits):
        if direct and part == 1:
            after = (
                *grad_space_parts,
                *time_in_sum.second(),
                *out_sum.first(),
                *contract_line.step(),
                *expand_line.step(),
            )
        grads, backs, gain_part, shift_part, own_sum = spatial_backward(
            gate(scalars, *after),
            frame_ups[part],
            frame_tokens[part],
            embed_own[first : first + many],
            gains[0:1],
            saved[part][1],
            saved[part][2],
            space_in,
        )
        gain_one, shift_one = gain_one + gain_part, shift_one + shift_part
        own_sums.append(own_sum)
        grad_space_parts.append(grads)
        back_parts.append((exchange(list(backs), direct), first))
    after = (*grad_space_parts,)
    if direct:
        time_in_line = LineSum(time_in_sum.total())
        after = (*grad_space_parts, *out_sum.second(), *contract_line.step(), *expand_line.step())
    space_in_parts = weight_grad(
        gate(scalars, *after),
        flat(jnp.concatenate([s[0] for s in saved], axis=0)),
        flat(jnp.concatenate(grad_space_parts, axis=0)),
        "space_in_grad",
    )

    own_sum = jnp.concatenate(own_sums, axis=0)
    grad_table = jnp.einsum(
        "fa,fd->ad", onehot, frame_sum[:, 0], precision=lax.Precision.HIGHEST
    ) + jnp.einsum("fa,fd->ad", onehot_own, own_sum[:, 0], precision=lax.Precision.HIGHEST)
    small_grads = jnp.concatenate(
        [
            grad_table,
            gain_one,
            gain_two,
            gain_three,
            shift_one,
            shift_two,
            shift_three,
            grad_wide_bias.reshape(-1, width),
            grad_out_bias,
        ],
        axis=0,
    )
    small_grads = sum_everywhere(small_grads) if direct else lax.psum(small_grads, ("seq", "tile"))
    input_grad = input_back(scalars, grad_space_sum, back_parts, share)

    if direct:
        space_in_sum = SeqSum(*space_in_parts)
        space_in_sum.first()
        out_line = LineSum(out_sum.total())
        time_in_line.step()
        expand_line.step()
        space_in_sum.second()
        out_line.step()
        time_in_line.step()
        space_in_line = LineSum(space_in_sum.total())
        out_line.step()
        time_in_line.step()
        out_line.step()
        for _ in range(tiles - 1):
            space_in_line.step()
        total_space_in, total_time_in, total_expand, total_contract = (
            line.sum for line in (space_in_line, time_in_line, expand_line, contract_line)
        )
        total_time_out, total_space_out = out_line.sum[:, :width], out_line.sum[:, width:]
    else:
        total_space_in, total_time_in, total_expand, total_contract = (
            plain_total(*parts)
            for parts in (space_in_parts, time_in_parts, expand_parts, contract_parts)
        )
        total_out = plain_total(*out_parts)
        total_time_out, total_space_out = total_out[:, :width], total_out[:, width:]

    here = lax.axis_index("seq")

    def own_lanes(array):
        return lax.dynamic_slice_in_dim(array, here * lanes, lanes, 1)

    wide_total = small_grads[kinds + 6 : -1].reshape(-1)
    wide_share = expand_bias.shape[0]
    return (
        outputs.reshape(inputs.shape),
        input_grad.reshape(inputs.shape),
        own_lanes(small_grads[:kinds]),
        total_space_in,
        total_space_out,
        total_time_in,
        total_time_out,
        total_expand,
        total_contract,
        lax.dynamic_slice_in_dim(wide_total, here * wide_share, wide_share, 0),
        own_lanes(small_grads[-1:]).reshape(-1),
        own_lanes(small_grads[kinds : kinds + 3]),
        own_lanes(small_grads[kinds + 3 : kinds + 6]),
    )


def solution(mesh):
    seq_first, seq_last = P("seq", None), P(None, "seq")
    stream = P("seq", None, "tile", None)
    return jax.shard_map(
        body,
        mesh=mesh,
        in_specs=(stream, seq_first, seq_first, stream, seq_last)
        + (seq_first,) * 6
        + (P("seq"), P("seq"), seq_last, seq_last),
        out_specs=(stream, stream, seq_last)
        + (seq_first,) * 6
        + (P("seq"), P("seq"), seq_last, seq_last),
        check_vma=False,
    )
```

```python
import functools
import math

import jax
import jax.numpy as jnp
from jax import lax
from jax.experimental import pallas as pl
from jax.experimental.pallas import tpu as pltpu
from jax.sharding import PartitionSpec as P

HEAD = 64
PAIR = 2 * HEAD
BLOCKS = 8
GROUP = 16
CHUNK = 1024
SET = 4
WIDE = 512
VMEM = 64000 * 1024

epsilon = 1e-05
masked_score = -1e30
score_scale = HEAD ** (-0.5)
f32 = jnp.float32
bf16 = jnp.bfloat16
ANY = pl.BlockSpec(memory_space=pl.ANY)


def dot_nn(left, right):
    return lax.dot_general(left, right, (((1,), (0,)), ((), ())), preferred_element_type=f32)


def dot_nt(left, right):
    return lax.dot_general(left, right, (((1,), (1,)), ((), ())), preferred_element_type=f32)


def dot_tn(left, right):
    return lax.dot_general(left, right, (((0,), (0,)), ((), ())), preferred_element_type=f32)


def flipped(block):
    return block.astype(f32).T.astype(block.dtype)


def norm_unit(hidden):
    centred = hidden - jnp.mean(hidden, axis=-1, keepdims=True)
    inverse = lax.rsqrt(jnp.mean(centred * centred, axis=-1, keepdims=True) + epsilon)
    return centred * inverse, inverse


def norm_back(upstream, unit, inverse, gain_row):
    scaled = upstream * gain_row
    mean_first = jnp.mean(scaled, axis=-1, keepdims=True)
    mean_second = jnp.mean(scaled * unit, axis=-1, keepdims=True)
    return inverse * (scaled - mean_first - unit * mean_second)


def column_sum(block):
    return jnp.sum(block, axis=0, keepdims=True)


def half_lanes(block, half):
    lanes = lax.broadcasted_iota(jnp.int32, block.shape, 1)
    return jnp.where((lanes < HEAD) == (half == 0), block, jnp.zeros_like(block))


def pair_rows(block):
    return jnp.concatenate([half_lanes(block, 0), half_lanes(block, 1)], axis=0)


def pick_lanes(stacked):
    size = stacked.shape[0] // 2
    lanes = lax.broadcasted_iota(jnp.int32, (size, stacked.shape[1]), 1)
    return jnp.where(lanes < HEAD, stacked[:size], stacked[size:])


def attend(query, key, value, mask):
    scores = dot_nt(pair_rows(query * jnp.asarray(score_scale, bf16)), key)
    if mask is not None:
        scores = jnp.where(mask, scores, masked_score)
    top = jnp.max(scores, axis=1, keepdims=True)
    powered = jnp.exp(scores - top)
    total = jnp.sum(powered, axis=1, keepdims=True)
    mixed = dot_nn(powered.astype(bf16), value) / total
    return pick_lanes(mixed).astype(bf16), top + jnp.log(total)


def attend_back(query, key, value, upstream, sums, mask):
    query = pair_rows(query * jnp.asarray(score_scale, bf16))
    upstream = pair_rows(upstream)
    scores = dot_nt(key, query)
    if mask is not None:
        scores = jnp.where(mask, scores, masked_score)
    soft = jnp.exp(scores - sums)
    grad_soft = dot_nt(value, upstream)
    inner = jnp.sum(soft * grad_soft, axis=0, keepdims=True)
    grad_scores = (soft * (grad_soft - inner)).astype(bf16)
    grad_value = dot_nn(soft.astype(bf16), upstream)
    grad_key = dot_nn(grad_scores, query)
    grad_query = pick_lanes(dot_tn(grad_scores, key)) * score_scale
    return grad_query.astype(bf16), grad_key.astype(bf16), grad_value.astype(bf16)


def lane_slices(index, width):
    base = pl.multiple_of(index * SET * PAIR, SET * PAIR)
    return [
        [pl.ds(base + (pair * PAIR + part * width), PAIR) for part in range(3)]
        for pair in range(SET)
    ]


def attend_set(index, width, load, store, mask, sums_store):
    columns = None
    for pair, lanes in enumerate(lane_slices(index, width)):
        out, sums = attend(*(load(lane) for lane in lanes), mask)
        store(lanes[0], out)
        size = out.shape[0]
        if columns is None:
            columns = jnp.zeros((size, PAIR), f32)
            spots = lax.broadcasted_iota(jnp.int32, columns.shape, 1)
        for half in (0, 1):
            part = sums[half * size : (half + 1) * size]
            columns = jnp.where(spots == 2 * pair + half, part, columns)
    sums_store(columns.T[: 2 * SET])


def attend_back_set(index, width, load, load_up, store, mask, sums):
    for pair, lanes in enumerate(lane_slices(index, width)):
        row = jnp.concatenate([sums[2 * pair : 2 * pair + 1], sums[2 * pair + 1 : 2 * pair + 2]], axis=1)
        grads = attend_back(*(load(lane) for lane in lanes), load_up(lanes[0]), row, mask)
        for lane, grad in zip(lanes, grads):
            store(lane, grad)


def weight_copies(scalars, places, refs, whole, sems, rows):
    copies = []
    for index, (place, ref) in enumerate(zip(places, refs)):
        start = pl.multiple_of((place ^ scalars[0]) * rows, 16)
        copies.append(
            pltpu.make_async_copy(ref, whole.at[pl.ds(start, ref.shape[0])], sems.at[index])
        )
    return copies


def call(kernel, grid, in_specs, out_specs, out_shape, scratch, flops, moved, name):
    return pl.pallas_call(
        kernel,
        out_shape=out_shape,
        grid_spec=pltpu.PrefetchScalarGridSpec(
            num_scalar_prefetch=1,
            grid=grid,
            in_specs=in_specs,
            out_specs=out_specs,
            scratch_shapes=scratch,
        ),
        compiler_params=pltpu.CompilerParams(vmem_limit_bytes=VMEM),
        cost_estimate=pl.CostEstimate(flops=flops, bytes_accessed=moved, transcendentals=0),
        name=name,
    )


def shape(dims, dtype=bf16):
    return jax.ShapeDtypeStruct(tuple(dims), dtype)


def full(dims):
    return pl.BlockSpec(tuple(dims), lambda i, s: (0,) * len(dims))


def rows_of(block):
    return block.reshape(block.shape[0] * block.shape[1], block.shape[2])


def spatial_forward(scalars, tokens, part, many, embed, gain, shift, weight):
    arrays, places, rows = weight
    tiles, _, cells, width = tokens.shape
    length, count = tiles * cells, len(arrays)
    heads, sets = width // HEAD, width // (PAIR * SET)

    def kernel(scalars_ref, *refs):
        token_ref, embed_ref, gain_ref, shift_ref, *refs = refs
        pieces, refs = refs[:count], refs[count:]
        normed_ref, proj_ref, mixed_ref, sums_ref, whole, sems = refs
        copies = weight_copies(scalars_ref, places, pieces, whole, sems, rows)
        for copy in copies:
            copy.start()
        for frame in range(many):
            hidden = rows_of(token_ref[:, frame]).astype(f32)
            unit, _ = norm_unit(hidden + embed_ref[frame])
            normed_ref[frame] = (unit * gain_ref[...] + shift_ref[...]).astype(bf16)
        for copy in copies:
            copy.wait()
        for start in range(0, 3 * width, CHUNK):
            out = dot_nn(rows_of(normed_ref[...]), whole[:, start : start + CHUNK])
            proj_ref[:, :, start : start + CHUNK] = out.astype(bf16).reshape(many, length, CHUNK)

        def run(index, carry):
            frame, lane_set = index // sets, index % sets

            def store(lane, value):
                mixed_ref[:, frame, :, lane] = value.reshape(tiles, cells, PAIR)

            def sums_store(value):
                spot = pl.multiple_of(lane_set * 2 * SET, 2 * SET)
                sums_ref[frame, pl.ds(spot, 2 * SET)] = value

            attend_set(
                lane_set, width, lambda lane: proj_ref[frame, :, lane], store, None, sums_store
            )
            return carry

        lax.fori_loop(0, many * sets, run, 0)

    return call(
        kernel,
        (1,),
        [
            pl.BlockSpec((tiles, many, cells, width), lambda i, s: (0, part, 0, 0)),
            pl.BlockSpec((many, 1, width), lambda i, s: (part, 0, 0)),
            full((1, width)),
            full((1, width)),
        ]
        + [ANY] * count,
        [
            full((many, length, width)),
            full((many, length, 3 * width)),
            full((tiles, many, cells, width)),
            full((many, heads, length)),
        ],
        [
            shape((many, length, width)),
            shape((many, length, 3 * width)),
            shape((tiles, many, cells, width)),
            shape((many, heads, length), f32),
        ],
        [pltpu.VMEM((width, 3 * width), bf16), pltpu.SemaphoreType.DMA((count,))],
        2 * many * length * width * (3 * width + 2 * length) * 2,
        20 << 20,
        "spatial_forward",
    )(scalars, tokens, embed, gain, shift, *arrays)


def spatial_backward(scalars, upstream, tokens, part, many, embed, gain, proj, sums, weight):
    arrays, places, rows = weight
    tiles, _, cells, width = tokens.shape
    length, count = tiles * cells, len(arrays)
    heads, sets = width // HEAD, width // (PAIR * SET)

    def kernel(scalars_ref, *refs):
        up_ref, token_ref, embed_ref, gain_ref, proj_ref, sums_ref, *refs = refs
        pieces, refs = refs[:count], refs[count:]
        grad_ref, back_ref, gain_grad, shift_grad, frame_sum, whole, sems = refs
        copies = weight_copies(scalars_ref, places, pieces, whole, sems, rows)
        for copy in copies:
            copy.start()

        def run(index, carry):
            frame, lane_set = index // sets, index % sets

            def store(lane, value):
                grad_ref[frame, :, lane] = value

            spot = pl.multiple_of(lane_set * 2 * SET, 2 * SET)
            attend_back_set(
                lane_set,
                width,
                lambda lane: proj_ref[frame, :, lane],
                lambda lane: rows_of(up_ref[:, frame, :, lane]),
                store,
                None,
                sums_ref[frame, pl.ds(spot, 2 * SET)],
            )
            return carry

        lax.fori_loop(0, many * sets, run, 0)
        for copy in copies:
            copy.wait()
        grad_normed = dot_nt(rows_of(grad_ref[...]), whole[...])
        gains, shifts = 0, 0
        for frame in range(many):
            hidden = rows_of(token_ref[:, frame]).astype(f32)
            unit, inverse = norm_unit(hidden + embed_ref[frame])
            grad = grad_normed[frame * length : (frame + 1) * length]
            back = norm_back(grad, unit, inverse, gain_ref[...])
            gains, shifts = gains + column_sum(grad * unit), shifts + column_sum(grad)
            frame_sum[frame] = column_sum(back)
            back_ref[:, frame] = back.astype(bf16).reshape(tiles, cells, width)
        gain_grad[...], shift_grad[...] = gains, shifts

    return call(
        kernel,
        (1,),
        [
            full((tiles, many, cells, width)),
            pl.BlockSpec((tiles, many, cells, width), lambda i, s: (0, part, 0, 0)),
            pl.BlockSpec((many, 1, width), lambda i, s: (part, 0, 0)),
            full((1, width)),
            full((many, length, 3 * width)),
            full((many, heads, length)),
        ]
        + [ANY] * count,
        [
            full((many, length, 3 * width)),
            full((tiles, many, cells, width)),
            full((1, width)),
            full((1, width)),
            full((many, 1, width)),
        ],
        [
            shape((many, length, 3 * width)),
            shape((tiles, many, cells, width)),
            shape((1, width), f32),
            shape((1, width), f32),
            shape((many, 1, width), f32),
        ],
        [pltpu.VMEM((width, 3 * width), bf16), pltpu.SemaphoreType.DMA((count,))],
        2 * many * length * width * (3 * width + 5 * length) * 2,
        24 << 20,
        "spatial_backward",
    )(scalars, upstream, tokens, embed, gain, proj, sums, *arrays)


def temporal_forward(scalars, tokens, embed, mixed_parts, share, gains, shifts, mask, middle):
    frames, cells, width = tokens.shape
    tiles, many = mixed_parts[0].shape[:2]
    count = len(mixed_parts)
    heads, sets, size = width // HEAD, width // (PAIR * SET), frames * GROUP
    groups = cells // GROUP
    cuts = (0, width, 4 * width, 5 * width)

    def kernel(scalars_ref, *refs):
        token_ref, embed_ref, *refs = refs
        part_refs, refs = refs[:count], refs[count:]
        gain_ref, shift_ref, mask_ref, middle_ref, *refs = refs
        outs, sums_ref, kept, refs = refs[:7], refs[7], refs[8:15], refs[15:]
        whole, sems, gathered, out_sems = refs
        space, first, normed, proj, mixed, second, last = kept
        copies = [
            pltpu.make_async_copy(
                middle_ref.at[:, start:stop], whole.at[:, start:stop], sems.at[index]
            )
            for index, (start, stop) in enumerate(zip(cuts, cuts[1:]))
        ]
        flushes = [
            pltpu.make_async_copy(ref, out, out_sems.at[index])
            for index, (ref, out) in enumerate(zip(kept, outs))
        ]
        for copy in copies:
            copy.start()
        for index, ref in enumerate(part_refs):
            for tile in range(tiles):
                start = tile * share + index * many
                gathered[start : start + many] = ref[tile]
        space[...] = gathered[:frames]
        flushes[0].start()
        copies[0].wait()
        hidden = rows_of(token_ref[...].astype(f32) + embed_ref[...])
        hidden = hidden + dot_nn(rows_of(space[...]), whole[:, :width])
        first[...] = hidden.reshape(first.shape)
        flushes[1].start()
        unit, _ = norm_unit(hidden)
        normed[...] = (unit * gain_ref[1:2] + shift_ref[1:2]).astype(bf16).reshape(normed.shape)
        flushes[2].start()
        copies[1].wait()
        for start in range(0, 3 * width, CHUNK):
            out = dot_nn(rows_of(normed[...]), whole[:, width + start : width + start + CHUNK])
            proj[:, :, start : start + CHUNK] = out.astype(bf16).reshape(frames, cells, CHUNK)
        flushes[3].start()
        allowed = mask_ref[...] > 0

        def run(index, carry):
            group, lane_set = index // sets, index % sets
            here = pl.ds(pl.multiple_of(group * GROUP, GROUP), GROUP)

            def store(lane, value):
                mixed[:, here, lane] = value.reshape(frames, GROUP, PAIR)

            def sums_store(value):
                spot = pl.multiple_of(lane_set * 2 * SET, 2 * SET)
                sums_ref[group, pl.ds(spot, 2 * SET)] = value

            attend_set(
                lane_set,
                width,
                lambda lane: rows_of(proj[:, here, lane]),
                store,
                allowed,
                sums_store,
            )
            return carry

        lax.fori_loop(0, groups * sets, run, 0)
        flushes[4].start()
        copies[2].wait()
        hidden = rows_of(first[...]) + dot_nn(rows_of(mixed[...]), whole[:, 4 * width :])
        second[...] = hidden.reshape(second.shape)
        flushes[5].start()
        unit, _ = norm_unit(hidden)
        last[...] = (unit * gain_ref[2:3] + shift_ref[2:3]).astype(bf16).reshape(last.shape)
        flushes[6].start()
        for flush in flushes:
            flush.wait()

    wide = (frames, cells, width)
    kept = [
        (wide, bf16),
        (wide, f32),
        (wide, bf16),
        ((frames, cells, 3 * width), bf16),
        (wide, bf16),
        (wide, f32),
        (wide, bf16),
    ]
    return call(
        kernel,
        (1,),
        [full(wide), full((frames, 1, width))]
        + [full(array.shape) for array in mixed_parts]
        + [full((3, width)), full((3, width)), full((2 * size, size)), ANY],
        [ANY] * 7 + [full((groups, heads, size))],
        [shape(*k) for k in kept] + [shape((groups, heads, size), f32)],
        [pltpu.VMEM(*k) for k in kept]
        + [
            pltpu.VMEM((width, 5 * width), bf16),
            pltpu.SemaphoreType.DMA((3,)),
            pltpu.VMEM((share * tiles, cells, width), bf16),
            pltpu.SemaphoreType.DMA((7,)),
        ],
        2 * frames * cells * width * (5 * width + 2 * size) * 2,
        40 << 20,
        "temporal_forward",
    )(scalars, tokens, embed, *mixed_parts, gains, shifts, mask, middle)


def temporal_backward(
    scalars, upstream, upstream_low, hidden, proj, sums, gains, mask, middle, tiles, share, count
):
    frames, cells, width = upstream.shape
    heads, sets, size = width // HEAD, width // (PAIR * SET), frames * GROUP
    groups, many = cells // GROUP, share // count
    cuts = (0, width, 4 * width, 5 * width)

    def kernel(scalars_ref, *refs):
        up_ref, low_ref, hidden_ref, proj_ref, sums_ref, gain_ref, mask_ref, *refs = refs
        middle_ref, grad_out, first_out, low_out, *refs = refs
        part_refs, refs = refs[:count], refs[count:]
        gain_grad, shift_grad, frame_sum, grads, first, first_low, *refs = refs
        whole, sems, mixed, out_sems = refs
        copies = [
            pltpu.make_async_copy(
                middle_ref.at[:, start:stop], whole.at[:, start:stop], sems.at[index]
            )
            for index, (start, stop) in enumerate(zip(cuts, cuts[1:]))
        ]
        flushes = [
            pltpu.make_async_copy(ref, out, out_sems.at[index])
            for index, (ref, out) in enumerate(
                ((grads, grad_out), (first, first_out), (first_low, low_out))
            )
        ]
        for copy in copies[::-1]:
            copy.start()
        copies[2].wait()
        out = dot_nt(rows_of(low_ref[...]), whole[:, 4 * width :])
        mixed[...] = out.astype(bf16).reshape(mixed.shape)
        allowed = mask_ref[...] > 0

        def run(index, carry):
            group, lane_set = index // sets, index % sets
            here = pl.ds(pl.multiple_of(group * GROUP, GROUP), GROUP)

            def store(lane, value):
                grads[:, here, lane] = value.reshape(frames, GROUP, PAIR)

            spot = pl.multiple_of(lane_set * 2 * SET, 2 * SET)
            attend_back_set(
                lane_set,
                width,
                lambda lane: rows_of(proj_ref[:, here, lane]),
                lambda lane: rows_of(mixed[:, here, lane]),
                store,
                allowed,
                sums_ref[group, pl.ds(spot, 2 * SET)],
            )
            return carry

        lax.fori_loop(0, groups * sets, run, 0)
        flushes[0].start()
        copies[1].wait()
        grad_normed = dot_nt(rows_of(grads[...]), whole[:, width : 4 * width])
        unit, inverse = norm_unit(rows_of(hidden_ref[...]))
        gain_grad[...] = column_sum(grad_normed * unit)
        shift_grad[...] = column_sum(grad_normed)
        out = rows_of(up_ref[...]) + norm_back(grad_normed, unit, inverse, gain_ref[1:2])
        out = out.reshape(first.shape)
        first[...] = out
        first_low[...] = out.astype(bf16)
        flushes[1].start()
        flushes[2].start()
        frame_sum[...] = jnp.sum(out, axis=1, keepdims=True)
        copies[0].wait()
        space = dot_nt(rows_of(first_low[...]), whole[:, :width]).astype(bf16)
        space = space.reshape(frames, cells, width)
        for index, ref in enumerate(part_refs):
            for tile in range(tiles):
                start = tile * share + index * many
                have = max(0, min(many, frames - start))
                if have:
                    ref[tile, :have] = space[start : start + have]
                if have < many:
                    ref[tile, have:] = jnp.zeros((many - have, cells, width), bf16)
        for flush in flushes:
            flush.wait()

    wide = (frames, cells, width)
    kept = [((frames, cells, 3 * width), bf16), (wide, f32), (wide, bf16)]
    outs = call(
        kernel,
        (1,),
        [full(wide)] * 3
        + [full((frames, cells, 3 * width)), full((groups, heads, size))]
        + [full((3, width)), full((size, 2 * size)), ANY],
        [ANY] * 3
        + [full((tiles, many, cells, width))] * count
        + [full((1, width)), full((1, width)), full((frames, 1, width))],
        [shape(*k) for k in kept]
        + [shape((tiles, many, cells, width))] * count
        + [shape((1, width), f32)] * 2
        + [shape((frames, 1, width), f32)],
        [pltpu.VMEM(*k) for k in kept]
        + [
            pltpu.VMEM((width, 5 * width), bf16),
            pltpu.SemaphoreType.DMA((3,)),
            pltpu.VMEM(wide, bf16),
            pltpu.SemaphoreType.DMA((3,)),
        ],
        2 * frames * cells * width * (5 * width + 5 * size) * 2,
        40 << 20,
        "temporal_backward",
    )(scalars, upstream, upstream_low, hidden, proj, sums, gains, mask, middle)
    return outs[0], outs[1], outs[2], outs[3 : 3 + count], *outs[3 + count :]


def expand_forward(scalars, normed, bias, weight):
    size, width = normed.shape
    hidden = weight.shape[1]
    root = math.sqrt(2 / math.pi)

    def kernel(scalars_ref, normed_ref, bias_ref, weight_ref, act_ref, slope_ref):
        value = dot_nn(normed_ref[...], weight_ref[...]) + bias_ref[...]
        square = value * value
        gate = 0.5 + 0.5 * jnp.tanh(value * (root + (root * 0.044715) * square))
        act = value * gate
        act_ref[...] = act.astype(bf16)
        slope = gate + act * (1.0 - gate) * (2 * root + (6 * root * 0.044715) * square)
        slope_ref[...] = slope.astype(bf16)

    def columns(lines):
        return pl.BlockSpec((lines, WIDE), lambda n, s: (0, n))

    return call(
        kernel,
        (hidden // WIDE,),
        [full((size, width)), columns(1), columns(width)],
        [columns(size)] * 2,
        [shape((size, hidden)), shape((size, hidden))],
        [],
        2 * size * width * hidden,
        25 << 20,
        "expand_forward",
    )(scalars, normed, bias, weight)


def expand_backward(scalars, upstream, slope, hidden, gain, expand, contract):
    size, width = upstream.shape
    inner = slope.shape[1]
    steps = 4
    chunk = inner // steps

    def kernel(scalars_ref, up_ref, slope_ref, hidden_ref, gain_ref, expand_ref, contract_ref, *refs):
        grad_ref, out_ref, low_ref, gain_grad, shift_grad, bias_grad, out_bias, total = refs
        grad = dot_nt(up_ref[...], contract_ref[...]) * slope_ref[...].astype(f32)
        grad_ref[...] = grad.astype(bf16)
        bias_grad[...] = column_sum(grad)
        part = dot_nt(grad_ref[...], expand_ref[...])

        @pl.when(pl.program_id(0) == 0)
        def _():
            total[...] = part

        @pl.when(pl.program_id(0) > 0)
        def _():
            total[...] += part

        @pl.when(pl.program_id(0) == steps - 1)
        def _():
            unit, inverse = norm_unit(hidden_ref[...])
            gain_grad[...] = column_sum(total[...] * unit)
            shift_grad[...] = column_sum(total[...])
            up = up_ref[...].astype(f32)
            out_bias[...] = column_sum(up)
            out = up + norm_back(total[...], unit, inverse, gain_ref[2:3])
            out_ref[...] = out
            low_ref[...] = out.astype(bf16)

    def columns(lines):
        return pl.BlockSpec((lines, chunk), lambda n, s: (0, n))

    once = pl.BlockSpec((size, width), lambda n, s: (0, 0), pipeline_mode=pl.Buffered(1))
    return call(
        kernel,
        (steps,),
        [
            once,
            columns(size),
            once,
            full((3, width)),
            columns(width),
            pl.BlockSpec((chunk, width), lambda n, s: (n, 0)),
        ],
        [columns(size), full((size, width)), full((size, width))]
        + [full((1, width)), full((1, width)), columns(1), full((1, width))],
        [
            shape((size, inner)),
            shape((size, width), f32),
            shape((size, width)),
            shape((1, width), f32),
            shape((1, width), f32),
            shape((1, inner), f32),
            shape((1, width), f32),
        ],
        [pltpu.VMEM((size, width), f32)],
        4 * size * width * inner,
        40 << 20,
        "expand_backward",
    )(scalars, upstream, slope, hidden, gain, expand, contract)


def contract_forward(scalars, act, hidden, bias, contract):
    size, inner = act.shape
    width = hidden.shape[1]
    steps = 4
    chunk = inner // steps

    def kernel(scalars_ref, act_ref, hidden_ref, bias_ref, contract_ref, out_ref, total):
        part = dot_nn(act_ref[...], contract_ref[...])

        @pl.when(pl.program_id(0) == 0)
        def _():
            total[...] = part + (hidden_ref[...] + bias_ref[...])

        @pl.when(pl.program_id(0) > 0)
        def _():
            total[...] += part

        @pl.when(pl.program_id(0) == steps - 1)
        def _():
            out_ref[...] = total[...].astype(bf16)

    return call(
        kernel,
        (steps,),
        [
            pl.BlockSpec((size, chunk), lambda n, s: (0, n)),
            full((size, width)),
            full((1, width)),
            pl.BlockSpec((chunk, width), lambda n, s: (n, 0)),
        ],
        [full((size, width))],
        [shape((size, width))],
        [pltpu.VMEM((size, width), f32)],
        2 * size * width * inner,
        20 << 20,
        "contract_forward",
    )(scalars, act, hidden, bias, contract)[0]


def contract_grad(scalars, left, right):
    size, height = left.shape
    width = right.shape[1]
    rows = height // 4

    def kernel(scalars_ref, left_ref, right_ref, out_ref):
        out_ref[...] = dot_tn(left_ref[...], right_ref[...]).astype(bf16)

    return call(
        kernel,
        (4,),
        [pl.BlockSpec((size, rows), lambda j, s: (0, j)), full((size, width))],
        [pl.BlockSpec((rows, width), lambda j, s: (j, 0))],
        [shape((height, width))],
        [],
        2 * size * height * width,
        (size * (height + width) + height * width) * 2,
        "contract_grad",
    )(scalars, left, right)[0]


def weight_grad(scalars, pairs, split, name):
    pairs = [(left, right) for left, right in pairs]
    lefts = [array for left, _ in pairs for array in left]
    rights = [array for _, right in pairs for array in right]
    height = lefts[0].shape[1]
    widths = [right[0].shape[1] for _, right in pairs]
    sizes = [sum(array.shape[0] for array in left) for left, _ in pairs]
    rows, half = height // BLOCKS, BLOCKS // 2
    chunk = CHUNK
    first = [sum(widths[:index]) // chunk for index in range(len(widths))]
    steps = sum(widths) // chunk

    def kernel(scalars_ref, *refs):
        left_refs, refs = refs[: len(lefts)], refs[len(lefts) :]
        right_refs, refs = refs[: len(rights)], refs[len(rights) :]
        out_refs, turned = refs[:-1], refs[-1]
        at = 0
        for index, (left, _) in enumerate(pairs):
            here = range(at, at + len(left))
            at += len(left)
            last = first[index] + widths[index] // chunk

            @pl.when(pl.program_id(0) == first[index])
            def _(here=here):
                for spot in range(BLOCKS):
                    lanes = pl.ds(spot * rows, rows)
                    if split:
                        owner = 2 * (spot % half) + spot // half
                        start = (owner ^ scalars_ref[0]) * rows
                        lanes = pl.ds(pl.multiple_of(start, rows), rows)
                    start = 0
                    for part in here:
                        ref = left_refs[part]
                        stop = start + ref.shape[0]
                        turned[spot * rows : (spot + 1) * rows, start:stop] = flipped(ref[:, lanes])
                        start = stop

            @pl.when((pl.program_id(0) >= first[index]) & (pl.program_id(0) < last))
            def _(here=here):
                start, out = 0, None
                for part in here:
                    ref = right_refs[part]
                    stop = start + ref.shape[0]
                    term = dot_nn(turned[:, start:stop], ref[...])
                    out = term if out is None else out + term
                    start = stop
                out = out.astype(bf16)
                if split:
                    out_refs[0][...] = out[: half * rows]
                    out_refs[1][...] = out[half * rows :]
                else:
                    out_refs[0][...] = out

    def right_spec(array, index):
        last = widths[index] // chunk - 1
        start = first[index]
        return pl.BlockSpec(
            (array.shape[0], chunk), lambda n, s: (0, jnp.clip(n - start, 0, last))
        )

    lines = half * rows if split else height
    count = 2 if split else 1
    return call(
        kernel,
        (steps,),
        [full(array.shape) for array in lefts]
        + [right_spec(array, index) for index, (_, right) in enumerate(pairs) for array in right],
        [pl.BlockSpec((lines, chunk), lambda n, s: (0, n))] * count,
        [shape((lines, sum(widths)))] * count,
        [pltpu.VMEM((height, max(sizes)), bf16)],
        2 * height * sum(size * width for size, width in zip(sizes, widths)),
        sum(array.size * 2 for array in lefts + rights) + height * sum(widths) * 2,
        name,
    )(scalars, *lefts, *rights)


def input_back(scalars, upstream, back_parts, share):
    frames, cells, width = upstream.shape
    tiles, many = back_parts[0].shape[:2]
    count = len(back_parts)

    def kernel(scalars_ref, up_ref, *refs):
        part_refs, (out_ref,) = refs[:count], refs[count:]
        for index, ref in enumerate(part_refs):
            for tile in range(tiles):
                start = tile * share + index * many
                have = max(0, min(many, frames - start))
                if have:
                    out = up_ref[start : start + have] + ref[tile, :have].astype(f32)
                    out_ref[start : start + have] = out.astype(bf16)

    spec = pl.BlockSpec((frames, GROUP, width), lambda g, s: (0, g, 0))
    part_spec = pl.BlockSpec((tiles, many, GROUP, width), lambda g, s: (0, 0, g, 0))
    return call(
        kernel,
        (cells // GROUP,),
        [spec] + [part_spec] * count,
        [spec],
        [shape(upstream.shape)],
        [],
        0,
        8 * frames * cells * width,
        "input_back",
    )(scalars, upstream, *back_parts)[0]


CORE, XCHIP, YCHIP = 1, 2, 4


def gate(value, *after):
    return lax.optimization_barrier((value, after))[0]


def across(array, flip):
    return lax.ppermute(array, "seq", [(i, i ^ flip) for i in range(BLOCKS)])


def gather_pieces(shard, small, tokens):
    chips = [(shard, 0), (across(shard, XCHIP), XCHIP), (across(shard, YCHIP), YCHIP)]
    chips.append((across(gate(shard, small), XCHIP | YCHIP), XCHIP | YCHIP))
    pieces = chips + [(across(gate(array, tokens), CORE), owner | CORE) for array, owner in chips]
    return [p[0] for p in pieces], [p[1] for p in pieces], shard.shape[0]


def exchange(array):
    return lax.all_to_all(array, "tile", 0, 0)


def core_sum(keep, received):
    return (keep.astype(f32) + received.astype(f32)).astype(bf16).reshape(4, -1, keep.shape[1])


def chip_parts(blocks):
    flips = (XCHIP, YCHIP, XCHIP | YCHIP)
    return [across(blocks[spot + 1], flip) for spot, flip in enumerate(flips)]


def chip_sum(blocks, parts):
    total = blocks[0].astype(f32)
    for part in parts:
        total = total + part.astype(f32)
    return total.astype(bf16)


def toward(array, pairs):
    return lax.ppermute(array, "tile", pairs)


class LineSum:
    def __init__(self, block):
        self.block = block
        self.first = toward(block, [(0, 1), (3, 2)])

    def middle(self):
        self.near = (self.block.astype(f32) + self.first.astype(f32)).astype(bf16)
        self.second = toward(self.near, [(1, 2), (2, 1)])
        return self.near

    def last(self):
        self.sum = (self.near.astype(f32) + self.second.astype(f32)).astype(bf16)
        self.third = toward(self.sum, [(1, 0), (2, 3)])
        return self.sum

    def total(self):
        tile = lax.axis_index("tile")
        return jnp.where((tile == 1) | (tile == 2), self.sum, self.third).astype(f32)


def sum_everywhere(array):
    for flip in (CORE, XCHIP, YCHIP):
        array = array + across(array, flip)
    for flip in (1, 2):
        array = array + lax.ppermute(array, "tile", [(i, i ^ flip) for i in range(4)])
    return array


def body(
    inputs,
    actions,
    segments,
    cotangent,
    action_table,
    spatial_inward,
    spatial_outward,
    temporal_inward,
    temporal_outward,
    expand_weight,
    contract_weight,
    expand_bias,
    contract_bias,
    norm_gain,
    norm_shift,
):
    seqs, tiles = lax.axis_size("seq"), lax.axis_size("tile")
    direct = seqs == BLOCKS and tiles == 4
    _, frames, cells, width = inputs.shape
    share = -(-frames // tiles)
    count = 2 if share % 2 == 0 else 1
    many = share // count
    kinds = action_table.shape[0]
    lanes = action_table.shape[1]
    me = lax.axis_index("seq").astype(jnp.int32) if direct else jnp.int32(0)
    scalars = me.reshape(1)

    tokens = inputs[0]
    padded = jnp.pad(tokens, ((0, share * tiles - frames), (0, 0), (0, 0)))
    frame_tokens = exchange(padded.reshape(tiles, share, cells, width))

    small = jnp.concatenate(
        [
            action_table,
            norm_gain,
            norm_shift,
            expand_bias.reshape(-1, lanes),
            contract_bias.reshape(1, lanes),
        ],
        axis=0,
    )
    small = lax.all_gather(small, "seq", axis=0)
    small = small.astype(f32)

    def joined(start, stop):
        return small[:, start:stop].transpose(1, 0, 2).reshape(stop - start, -1)

    table = joined(0, kinds)
    gains = joined(kinds, kinds + 3)
    shifts = joined(kinds + 3, kinds + 6)
    wide_bias = small[:, kinds + 6 : -1].reshape(1, -1)
    out_bias = small[:, -1].reshape(1, -1)

    def gathered(shard):
        return lax.all_gather(shard, "seq", axis=0, tiled=True)

    middle = jnp.concatenate([spatial_outward, temporal_inward, temporal_outward], axis=1)
    if direct:
        space_in = gather_pieces(spatial_inward, small, frame_tokens)
        middle = gathered(gate(middle, *space_in[0][1:3]))
        expand = gathered(gate(expand_weight, *space_in[0][4:]))
    else:
        space_in = ([gathered(spatial_inward)], [0], width // BLOCKS)
        middle, expand = gathered(middle), gathered(expand_weight)

    onehot = (actions[0][:, None] == jnp.arange(kinds, dtype=jnp.int32)[None, :]).astype(f32)
    embed = jnp.dot(onehot, table, precision=lax.Precision.HIGHEST)
    onehot_own = lax.dynamic_slice_in_dim(
        jnp.pad(onehot, ((0, share * tiles - frames), (0, 0))),
        lax.axis_index("tile") * share,
        share,
        0,
    )
    embed_own = jnp.dot(onehot_own, table, precision=lax.Precision.HIGHEST)
    embed, embed_own = embed[:, None, :], embed_own[:, None, :]

    index = jnp.arange(frames * GROUP, dtype=jnp.int32)
    frame_of, place_of = index // GROUP, index % GROUP
    ids = jnp.repeat(segments[0], GROUP)
    mask = (
        (place_of[:, None] == place_of[None, :])
        & (frame_of[:, None] >= frame_of[None, :])
        & (ids[:, None] == ids[None, :])
    ).astype(f32)
    mask_rows = jnp.concatenate([mask, mask], axis=0)
    mask_lanes = jnp.concatenate([mask.T, mask.T], axis=1)

    saved, mixed_parts = [], []
    for part in range(count):
        normed, proj, mixed, sums = spatial_forward(
            scalars, frame_tokens, part, many, embed_own, gains[0:1], shifts[0:1], space_in
        )
        saved.append((normed, proj, sums))
        mixed_parts.append(exchange(mixed))
    contract = gathered(gate(contract_weight, mixed))
    (
        space_rows,
        space_sum,
        normed_two,
        time_proj,
        time_mixed,
        time_sum,
        normed_three,
        time_sums,
    ) = temporal_forward(
        scalars, tokens, embed, mixed_parts, share, gains, shifts, mask_rows, middle
    )

    def flat(array):
        return array.reshape(-1, array.shape[-1])

    upstream = flat(cotangent[0])
    act, slope = expand_forward(scalars, flat(normed_three), wide_bias, expand)
    grad_contract = contract_grad(scalars, act, upstream)
    contract_block = lax.psum_scatter(grad_contract, "seq", scatter_dimension=0, tiled=True)
    (
        grad_hidden,
        grad_time_sum,
        time_low,
        gain_three,
        shift_three,
        grad_wide_bias,
        grad_out_bias,
    ) = expand_backward(
        gate(scalars, grad_contract), upstream, slope, flat(time_sum), gains, expand, contract
    )
    grad_expand = weight_grad(
        scalars, [([flat(normed_three)], [grad_hidden])], False, "expand_grad"
    )[0]
    expand_block = lax.psum_scatter(grad_expand, "seq", scatter_dimension=0, tiled=True)

    (
        grad_time_proj,
        grad_space_sum,
        space_low,
        space_ups,
        gain_two,
        shift_two,
        frame_sum,
    ) = temporal_backward(
        gate(scalars, grad_expand),
        grad_time_sum.reshape(frames, cells, width),
        time_low.reshape(frames, cells, width),
        space_sum,
        time_proj,
        time_sums,
        gains,
        mask_lanes,
        middle,
        tiles,
        share,
        count,
    )
    frame_ups = [exchange(ups) for ups in space_ups]
    time_parts = weight_grad(
        gate(scalars, grad_space_sum),
        [
            ([flat(time_mixed)], [time_low]),
            ([flat(space_rows)], [flat(space_low)]),
            ([flat(normed_two)], [flat(grad_time_proj)]),
        ],
        direct,
        "time_grad",
    )
    back_parts, grad_space_parts = [], []
    gain_one = shift_one = 0
    own_sums = []
    after = time_parts
    if direct:
        time_received = across(time_parts[1], CORE)
        after = (*time_parts, expand_block)
    for part in range(count):
        grads, backs, gain_part, shift_part, own_sum = spatial_backward(
            gate(scalars, *after),
            frame_ups[part],
            frame_tokens,
            part,
            many,
            embed_own,
            gains[0:1],
            saved[part][1],
            saved[part][2],
            space_in,
        )
        gain_one, shift_one = gain_one + gain_part, shift_one + shift_part
        own_sums.append(own_sum)
        grad_space_parts.append(grads)
        back_parts.append(exchange(backs))
        after = (grads,)
        if direct and part == 0:
            time_blocks = core_sum(gate(time_parts[0], grads), time_received)
            contract_line = LineSum(gate(contract_block, grads))
            time_chips = chip_parts(time_blocks)
            after = (grads, time_blocks)
    space_in_parts = weight_grad(
        gate(scalars, *after),
        [([flat(s[0]) for s in saved], [flat(g) for g in grad_space_parts])],
        direct,
        "space_in_grad",
    )
    after = space_in_parts
    if direct:
        space_received = across(space_in_parts[1], CORE)
        contract_line.block = gate(contract_line.block, *space_in_parts)
        expand_line = LineSum(gate(expand_block, contract_line.middle()))
        after = (*space_in_parts, expand_line.block)
    outputs = contract_forward(gate(scalars, *after), act, flat(time_sum), out_bias, contract)

    own_sum = jnp.concatenate(own_sums, axis=0)
    grad_table = jnp.einsum(
        "fa,fd->ad", onehot, frame_sum[:, 0], precision=lax.Precision.HIGHEST
    ) + jnp.einsum("fa,fd->ad", onehot_own, own_sum[:, 0], precision=lax.Precision.HIGHEST)
    small_grads = jnp.concatenate(
        [
            grad_table,
            gain_one,
            gain_two,
            gain_three,
            shift_one,
            shift_two,
            shift_three,
            grad_wide_bias.reshape(-1, width),
            grad_out_bias,
        ],
        axis=0,
    )
    small_grads = sum_everywhere(small_grads) if direct else lax.psum(small_grads, ("seq", "tile"))

    input_grad = input_back(scalars, grad_space_sum, back_parts, share)

    if direct:
        space_blocks = core_sum(gate(space_in_parts[0], outputs), space_received)
        space_chips = chip_parts(space_blocks)
        time_line = LineSum(chip_sum(gate(time_blocks, space_blocks), time_chips))
        contract_line.last()
        expand_line.middle()
        expand_line.last()
        time_line.middle()
        time_line.last()
        space_line = LineSum(chip_sum(space_blocks, space_chips))
        space_line.middle()
        space_line.last()
        total_contract, total_expand, total_time, total_space_in = (
            line.total() for line in (contract_line, expand_line, time_line, space_line)
        )
    else:

        def plain_total(array):
            shard = lax.psum_scatter(array, "seq", scatter_dimension=0, tiled=True)
            return lax.psum(shard, "tile").astype(f32)

        total_contract, total_expand = (
            lax.psum(block, "tile").astype(f32) for block in (contract_block, expand_block)
        )
        total_time, total_space_in = plain_total(time_parts[0]), plain_total(space_in_parts[0])

    here = lax.axis_index("seq")

    def own_lanes(array):
        return lax.dynamic_slice_in_dim(array, here * lanes, lanes, 1)

    wide_total = small_grads[kinds + 6 : -1].reshape(-1)
    wide_share = expand_bias.shape[0]
    return (
        outputs.reshape(inputs.shape),
        input_grad.reshape(inputs.shape),
        own_lanes(small_grads[:kinds]),
        total_space_in,
        total_time[:, width : 2 * width],
        total_time[:, 2 * width :],
        total_time[:, :width],
        total_expand,
        total_contract,
        lax.dynamic_slice_in_dim(wide_total, here * wide_share, wide_share, 0),
        own_lanes(small_grads[-1:]).reshape(-1),
        own_lanes(small_grads[kinds : kinds + 3]),
        own_lanes(small_grads[kinds + 3 : kinds + 6]),
    )


def solution(mesh):
    seq_first, seq_last = P("seq", None), P(None, "seq")
    stream = P("seq", None, "tile", None)
    return jax.shard_map(
        body,
        mesh=mesh,
        in_specs=(stream, seq_first, seq_first, stream, seq_last)
        + (seq_first,) * 6
        + (P("seq"), P("seq"), seq_last, seq_last),
        out_specs=(stream, stream, seq_last)
        + (seq_first,) * 6
        + (P("seq"), P("seq"), seq_last, seq_last),
        check_vma=False,
    )
```
